512 devices in a mesh: phase: 16 (over z, core), rows: 32 (over y, x).
Axes of the slice: x: 4, y: 8, z: 8, core: 2. Of those that a mesh axis runs over, the one named last changes fastest.
Arguments:
- start: bfloat16 [16, 32768, 256], P('phase', 'rows')
- blocks: bfloat16 [16, 256, 4, 128, 128], P('phase', 'rows')
- cols: int32 [16, 256, 4], P('phase', 'rows'), may hold values from 0 to 255, as said below
- counts: int32 [16, 256], P('phase', 'rows'), may hold values from 1 to 4, as said below
Outputs:
- basis: float32 [16, 32768, 256], P('phase', 'rows')
- factor: float32 [16, 256, 256], P('phase')
The draws below stay inside these ranges and needn't reach their ends.
Inputs may be any that keep to these rules, and one draw needn't show every extreme that they name: cols[q, i, 0] = i; the other slots of block row i name distinct block rows (i + o) mod 256 with 1 <= |o| <= 2. Block row i of section q uses its first counts[q, i] slots; every section has a block row that uses all 4.
All inputs are finite; a program needn't handle non-finite values.
Results may differ from the reference program's by a relative error of at most 0.012.
Values may be sent and summed in bfloat16 or wider, within the bound.
No kernel may reach another device: no remote copies, remote signals or barrier semaphores. Data moves between devices by JAX's collectives and lax.ppermute only.
A program may use at most 64 MiB of HBM per device.

```python
import jax
import jax.numpy as jnp
from jax import lax

BS = 128
K = 256
HB = 2
MAXB = 4
PHASES = 16
NBR = 256
STATES = 32768


def draw_start(key, part):
    key_a = jax.random.fold_in(jax.random.fold_in(key, 3), 0)
    row_index = jnp.arange(STATES, dtype=jnp.float32)
    row_rise = jnp.exp(jnp.log(3.0) * row_index / STATES)[None, :, None]
    values = jnp.clip(jax.random.normal(key_a, (PHASES, STATES, K), jnp.float32), -5.0, 5.0) * row_rise
    return values.astype(jnp.bfloat16)


def draw_blocks(key, part):
    key_a, key_b = jax.random.split(jax.random.fold_in(key, 11), 2)
    shape = (PHASES, NBR, MAXB, BS, BS)
    spread = 0.5 / jnp.sqrt(jnp.float32(BS * MAXB))
    noise_part = jnp.clip(jax.random.normal(key_a, shape, jnp.float32), -4.0, 4.0) * spread
    diagonal_scale = jnp.exp(jax.random.uniform(key_b, (PHASES, NBR, 1, BS, 1), jnp.float32, jnp.log(0.6), jnp.log(1.6)))
    identity_mask = jnp.arange(BS)[:, None] == jnp.arange(BS)[None, :]
    first_slot = (jnp.arange(MAXB) == 0)[:, None, None]
    diagonal_part = jnp.where(identity_mask[None, None, None, :, :] & first_slot[None, None, :, :, :], diagonal_scale, 0.0)
    return (noise_part + diagonal_part).astype(jnp.bfloat16)


def draw_cols(key, part):
    key_a = jax.random.fold_in(key, 5)
    scores = jax.random.randint(key_a, (PHASES, NBR, 2 * HB), 0, 2 ** 20) * (2 * HB) + jnp.arange(2 * HB, dtype=jnp.int32)
    chosen = jnp.argsort(scores, axis=-1, stable=True)[:, :, :MAXB - 1].astype(jnp.int32)
    offsets = jnp.where(chosen < HB, chosen - HB, chosen - HB + 1)
    row_index = jnp.arange(NBR, dtype=jnp.int32)[None, :, None]
    others = jnp.mod(row_index + offsets, NBR)
    diagonal_col = jnp.broadcast_to(row_index, (PHASES, NBR, 1))
    return jnp.concatenate([diagonal_col, others], axis=-1).astype(jnp.int32)


def draw_counts(key, part):
    key_a, key_b = jax.random.split(jax.random.fold_in(key, 7), 2)
    base_draw = jax.random.randint(key_a, (PHASES, NBR), 1, MAXB + 1)
    full_row = jax.random.randint(key_b, (PHASES, 1), 0, NBR)
    row_index = jnp.arange(NBR, dtype=jnp.int32)[None, :]
    return jnp.where(row_index == full_row, MAXB, base_draw).astype(jnp.int32)


def setup_inputs(seed: int = 0) -> dict:
    streams_of = jax.random.split(jax.random.key(seed), 5)
    start = draw_start(jax.random.fold_in(streams_of[4], 71), 0)
    blocks = draw_blocks(jax.random.fold_in(streams_of[4], 71), 0)
    cols = draw_cols(jax.random.fold_in(streams_of[4], 71), 0)
    counts = draw_counts(jax.random.fold_in(streams_of[4], 71), 0)
    return {"start": start, "blocks": blocks, "cols": cols, "counts": counts}


def section_apply(section_item):
    section_blocks, section_cols, section_counts, travel = section_item
    row_tiles = travel.reshape(STATES // BS, BS, K)
    picked = row_tiles[section_cols].astype(jnp.float32)
    live_slots = jnp.arange(MAXB, dtype=jnp.int32)[None, :] < section_counts[:, None]
    kept_blocks = jnp.where(live_slots[:, :, None, None], section_blocks.astype(jnp.float32), jnp.float32(0.0))
    applied = jnp.einsum('ijab,ijbk->iak', kept_blocks, picked)
    return applied.reshape(STATES, K).astype(jnp.bfloat16)

def finish(travel):
    gram_term = jnp.dot(travel.T.astype(jnp.float32), travel.astype(jnp.float32), preferred_element_type=jnp.float32)
    gram_matrix = gram_term / STATES
    lower_factor = jnp.linalg.cholesky(gram_matrix)
    basis_out = jax.scipy.linalg.solve_triangular(lower_factor, travel.astype(jnp.float32).T, lower=True).T
    return (basis_out, lower_factor.T)

def reference(start, blocks, cols, counts):

    def advance(travel, offset_turn):
        aligned = jnp.roll(travel, offset_turn, axis=0)
        applied = lax.map(section_apply, (blocks, cols, counts, aligned))
        return (jnp.roll(applied, -offset_turn, axis=0), jnp.int32(0))
    arrived, unused = lax.scan(advance, start, jnp.arange(PHASES, dtype=jnp.int32))
    basis, factor = lax.map(finish, arrived)
    return (basis, factor)
```

```python
import jax
import jax.numpy as jnp
from jax import lax
from jax.experimental import pallas as pl
from jax.experimental.pallas import tpu as pltpu
from jax.sharding import PartitionSpec as P

HB = 2
NB = 16

def factor_kernel(gram_ref, arrived_ref, basis_ref, factor_ref, a_ref, w_ref):
    size = gram_ref.shape[0]
    a_ref[...] = gram_ref[...]
    row_i = lax.broadcasted_iota(jnp.int32, (size, size), 0)
    col_i = lax.broadcasted_iota(jnp.int32, (size, size), 1)
    w_ref[...] = jnp.where(row_i == col_i, 1.0, 0.0)
    lanes = 128
    sub = lax.broadcasted_iota(jnp.int32, (NB, lanes), 0)
    wide_row = lax.broadcasted_iota(jnp.int32, (NB, size), 0)
    wide_col = lax.broadcasted_iota(jnp.int32, (NB, size), 1)
    for first in range(0, size, NB):
        panel = a_ref[first : first + NB, :]
        other = w_ref[first : first + NB, :]
        columns = [
            jnp.broadcast_to(panel[:, first + k : first + k + 1], (NB, lanes))
            for k in range(NB)
        ]
        pivots = jnp.zeros((NB, lanes), jnp.float32)
        for j in range(NB):
            column = columns[j]
            pivot = jnp.broadcast_to(column[j : j + 1, :], (NB, lanes))
            pivots = jnp.where(sub == j, pivot, pivots)
            if j == NB - 1:
                break
            scaled = jnp.where(sub > j, column / pivot, 0.0)
            for k in range(j + 1, NB):
                columns[k] = columns[k] - scaled * jnp.broadcast_to(
                    column[k : k + 1, :], (NB, lanes)
                )
            both = jnp.concatenate([scaled] * (size // lanes), axis=1)
            panel = panel - both * jnp.broadcast_to(panel[j : j + 1, :], (NB, size))
            other = other - both * jnp.broadcast_to(other[j : j + 1, :], (NB, size))
        scale = 1.0 / jnp.sqrt(pivots)
        both = jnp.concatenate([scale] * (size // lanes), axis=1)
        upper = jnp.where(wide_col >= wide_row + first, panel * both, 0.0)
        other = other * both
        factor_ref[first : first + NB, :] = upper
        w_ref[first : first + NB, :] = other
        rest = first + NB
        if rest < size:
            right = jnp.concatenate([upper, other], axis=1)
            change = lax.dot_general(
                upper, right, (((0,), (0,)), ((), ())),
                preferred_element_type=jnp.float32, precision=lax.Precision.HIGHEST,
            )
            a_ref[rest:, :] = a_ref[rest:, :] - change[rest:, :size]
            w_ref[rest:, :] = w_ref[rest:, :] - change[rest:, size:]
    w = w_ref[...]
    high = w.astype(jnp.bfloat16)
    low = (w - high.astype(jnp.float32)).astype(jnp.bfloat16)
    dims = (((1,), (1,)), ((), ()))
    for piece in range(0, arrived_ref.shape[0], 256):
        rows = arrived_ref[piece : piece + 256, :]
        basis_ref[piece : piece + 256, :] = lax.dot_general(
            rows, high, dims, preferred_element_type=jnp.float32
        ) + lax.dot_general(rows, low, dims, preferred_element_type=jnp.float32)

def finish(gram, arrived):
    size = gram.shape[0]
    vmem = pl.BlockSpec(memory_space=pltpu.VMEM)
    return pl.pallas_call(
        factor_kernel,
        out_shape=(
            jax.ShapeDtypeStruct(arrived.shape, jnp.float32),
            jax.ShapeDtypeStruct((size, size), jnp.float32),
        ),
        in_specs=[vmem, vmem],
        out_specs=(vmem, vmem),
        scratch_shapes=[pltpu.VMEM((size, size), jnp.float32), pltpu.VMEM((size, size), jnp.float32)],
        name="factor_solve",
    )(gram, arrived)


def sum_over_rows(term):
    owners = lax.axis_size("rows")
    size = term.shape[0]
    pieces = term.reshape(owners, size // owners, size)
    pieces = lax.all_to_all(pieces, "rows", 0, 0, tiled=True)
    mine = jnp.sum(pieces.astype(jnp.float32), axis=0, keepdims=True)
    copies = jnp.broadcast_to(mine, (owners, size // owners, size))
    return lax.all_to_all(copies, "rows", 0, 0, tiled=True).reshape(size, size)


def with_halo(array, sides, width):
    for axis, dim in sides:
        peers, length = (lax.axis_size(axis), array.shape[dim])
        up = [(i, (i + 1) % peers) for i in range(peers)]
        down = [(j, i) for i, j in up]
        last = lax.slice_in_dim(array, length - width, length, axis=dim)
        leading = lax.slice_in_dim(array, 0, width, axis=dim)
        before = lax.ppermute(last, axis, up)
        after = lax.ppermute(leading, axis, down)
        array = jnp.concatenate([before, array, after], axis=dim)
    return array


def passed_along(value, axis, steps):
    count = lax.axis_size(axis)
    pairs = [(source, (source + steps) % count) for source in range(count)]
    return lax.ppermute(value, axis, pairs)


def body(start, blocks, cols, counts):
    block_rows = blocks.shape[1]
    slot_count = blocks.shape[2]
    tile_size = blocks.shape[3]
    rows_here = start.shape[1]
    owners = lax.axis_size("rows")
    sections = lax.axis_size("phase")
    total_blocks = block_rows * owners
    first_block = lax.axis_index("rows") * block_rows
    local_index = jnp.mod(cols[0] - first_block + HB, total_blocks)
    live_slots = jnp.arange(slot_count, dtype=jnp.int32)[None, :] < counts[0][:, None]
    zero_value = jnp.zeros((), jnp.bfloat16)
    kept_blocks = jnp.where(live_slots[:, :, None, None], blocks[0], zero_value)
    rim_rows = HB * tile_size

    def advance(current):
        columns = current.shape[1]
        extended = with_halo(current, (("rows", 0),), rim_rows)
        row_tiles = extended.reshape(block_rows + 2 * HB, tile_size, columns)
        picked = row_tiles[local_index]
        product = jnp.einsum(
            "ijab,ijbk->iak", kept_blocks, picked, preferred_element_type=jnp.float32
        )
        return product.reshape(rows_here, columns).astype(jnp.bfloat16)

    def turn_one(turn_index, current):
        return passed_along(advance(current), "phase", 1)

    arrived = lax.fori_loop(0, sections, turn_one, start[0])
    gram_term = lax.dot_general(
        arrived, arrived, (((0,), (0,)), ((), ())), preferred_element_type=jnp.float32
    )
    gram_total = sum_over_rows(gram_term.astype(jnp.bfloat16)) / (rows_here * owners)
    basis_out, upper_factor = finish(gram_total, arrived)
    return (basis_out[None], upper_factor[None])


def solution(mesh):
    placed = (
        P("phase", "rows", None),
        P("phase", "rows", None, None, None),
        P("phase", "rows", None),
        P("phase", "rows"),
    )
    return jax.shard_map(
        body,
        mesh=mesh,
        in_specs=placed,
        out_specs=(P("phase", "rows", None), P("phase", None, None)),
        check_vma=False,
    )
```

```python
import jax
import jax.numpy as jnp
from jax import lax
from jax.experimental import pallas as pl
from jax.experimental.pallas import tpu as pltpu
from jax.sharding import PartitionSpec as P

HB = 2
TILE = 128
HALF = 4 * TILE
OPS = 16 * TILE
DEAD = 7

def visit_kernel(cur, ra, rb, first, second, out, wide, mid):
    for n in range(4):
        wide[(3 - n) * TILE : (4 - n) * TILE, :] = ra[n * TILE : (n + 1) * TILE, :]
        wide[(15 - n) * TILE : (16 - n) * TILE, :] = rb[n * TILE : (n + 1) * TILE, :]
    wide[4 * TILE : 12 * TILE, :] = cur[...]
    zero = jnp.zeros((TILE, cur.shape[1]), cur.dtype)
    wide[16 * TILE :, :] = zero
    mid[12 * TILE :, :] = zero

    def table_of(ref, start, count):
        return ref[start : start + count, :TILE].astype(jnp.float32).astype(jnp.int32)

    def row(ops, base, table, line, source, centre, sign, nothing):
        def block(j):
            if j == 0:
                return source[centre * TILE : (centre + 1) * TILE, :]
            value = jnp.max(table[line + j : line + j + 1, :])
            place = jnp.where(value == DEAD, nothing, centre + sign * (value - 2))
            return source[pl.ds(pl.multiple_of(place * TILE, TILE), TILE), :]

        total = None
        for pair in range(2):
            left = ops[base + pair * TILE : base + (pair + 1) * TILE, :]
            right = jnp.concatenate([block(2 * pair), block(2 * pair + 1)], axis=0)
            part = jnp.dot(left, right, preferred_element_type=jnp.float32)
            total = part if total is None else total + part
        return total.astype(out.dtype)

    near_a = table_of(ra, 2 * HALF, 16)
    near_b = table_of(rb, 2 * HALF, 16)
    own = table_of(first, OPS, 64)
    for n in range(2):
        c = -1 - n
        mid[(c + 2) * TILE : (c + 3) * TILE, :] = row(
            ra, HALF + n * 2 * TILE, near_a, n * 8, wide, c + 4, -1, 16
        )
        c = 9 - n
        mid[(c + 2) * TILE : (c + 3) * TILE, :] = row(
            rb, HALF + n * 2 * TILE, near_b, n * 8, wide, c + 4, -1, 16
        )
    for c in range(8):
        mid[(c + 2) * TILE : (c + 3) * TILE, :] = row(
            first, c * 2 * TILE, own, c * 8, wide, c + 4, 1, 16
        )
    other = table_of(second, OPS, 64)
    for c in range(8):
        out[c * TILE : (c + 1) * TILE, :] = row(
            second, c * 2 * TILE, other, c * 8, mid, c + 2, 1, 12
        )

def visit(cur, ra, rb, first, second):
    vmem = pl.BlockSpec(memory_space=pltpu.VMEM)
    columns = cur.shape[1]
    return pl.pallas_call(
        visit_kernel,
        out_shape=jax.ShapeDtypeStruct(cur.shape, cur.dtype),
        in_specs=[vmem] * 5,
        out_specs=vmem,
        scratch_shapes=[
            pltpu.VMEM((17 * TILE, columns), cur.dtype),
            pltpu.VMEM((13 * TILE, columns), cur.dtype),
        ],
        compiler_params=pltpu.CompilerParams(vmem_limit_bytes=24 * 1024 * 1024),
        cost_estimate=pl.CostEstimate(flops=700_000_000, bytes_accessed=4_000_000, transcendentals=0),
        name="two_steps",
    )(cur, ra, rb, first, second)


NB = 16

def factor_kernel(gram_ref, arrived_ref, basis_ref, factor_ref, a_ref, w_ref):
    size = gram_ref.shape[0]
    a_ref[...] = gram_ref[...]
    row_i = lax.broadcasted_iota(jnp.int32, (size, size), 0)
    col_i = lax.broadcasted_iota(jnp.int32, (size, size), 1)
    w_ref[...] = jnp.where(row_i == col_i, 1.0, 0.0)
    lanes = 128
    sub = lax.broadcasted_iota(jnp.int32, (NB, lanes), 0)
    wide_row = lax.broadcasted_iota(jnp.int32, (NB, size), 0)
    wide_col = lax.broadcasted_iota(jnp.int32, (NB, size), 1)
    for first in range(0, size, NB):
        panel = a_ref[first : first + NB, :]
        other = w_ref[first : first + NB, :]
        columns = [
            jnp.broadcast_to(panel[:, first + k : first + k + 1], (NB, lanes))
            for k in range(NB)
        ]
        pivots = jnp.zeros((NB, lanes), jnp.float32)
        for j in range(NB):
            column = columns[j]
            pivot = jnp.broadcast_to(column[j : j + 1, :], (NB, lanes))
            pivots = jnp.where(sub == j, pivot, pivots)
            if j == NB - 1:
                break
            scaled = jnp.where(sub > j, column / pivot, 0.0)
            for k in range(j + 1, NB):
                columns[k] = columns[k] - scaled * jnp.broadcast_to(
                    column[k : k + 1, :], (NB, lanes)
                )
            both = jnp.concatenate([scaled] * (size // lanes), axis=1)
            panel = panel - both * jnp.broadcast_to(panel[j : j + 1, :], (NB, size))
            other = other - both * jnp.broadcast_to(other[j : j + 1, :], (NB, size))
        scale = 1.0 / jnp.sqrt(pivots)
        both = jnp.concatenate([scale] * (size // lanes), axis=1)
        upper = jnp.where(wide_col >= wide_row + first, panel * both, 0.0)
        other = other * both
        factor_ref[first : first + NB, :] = upper
        w_ref[first : first + NB, :] = other
        rest = first + NB
        if rest < size:
            right = jnp.concatenate([upper, other], axis=1)
            change = lax.dot_general(
                upper, right, (((0,), (0,)), ((), ())),
                preferred_element_type=jnp.float32, precision=lax.Precision.HIGHEST,
            )
            a_ref[rest:, :] = a_ref[rest:, :] - change[rest:, :size]
            w_ref[rest:, :] = w_ref[rest:, :] - change[rest:, size:]
    w = w_ref[...]
    high = w.astype(jnp.bfloat16)
    low = (w - high.astype(jnp.float32)).astype(jnp.bfloat16)
    dims = (((1,), (1,)), ((), ()))
    for piece in range(0, arrived_ref.shape[0], 256):
        rows = arrived_ref[piece : piece + 256, :]
        basis_ref[piece : piece + 256, :] = lax.dot_general(
            rows, high, dims, preferred_element_type=jnp.float32
        ) + lax.dot_general(rows, low, dims, preferred_element_type=jnp.float32)

def finish(gram, arrived):
    size = gram.shape[0]
    vmem = pl.BlockSpec(memory_space=pltpu.VMEM)
    return pl.pallas_call(
        factor_kernel,
        out_shape=(
            jax.ShapeDtypeStruct(arrived.shape, jnp.float32),
            jax.ShapeDtypeStruct((size, size), jnp.float32),
        ),
        in_specs=[vmem, vmem],
        out_specs=(vmem, vmem),
        scratch_shapes=[pltpu.VMEM((size, size), jnp.float32), pltpu.VMEM((size, size), jnp.float32)],
        name="factor_solve",
    )(gram, arrived)


def sum_over_rows(term):
    owners = lax.axis_size("rows")
    size = term.shape[0]
    pieces = term.reshape(owners, size // owners, size)
    pieces = lax.all_to_all(pieces, "rows", 0, 0, tiled=True)
    mine = jnp.sum(pieces.astype(jnp.float32), axis=0, keepdims=True)
    copies = jnp.broadcast_to(mine, (owners, size // owners, size))
    return lax.all_to_all(copies, "rows", 0, 0, tiled=True).reshape(size, size)


def packed_operator(blocks, cols, counts, even):
    block_rows, slots, tile, unused = blocks.shape
    owners = lax.axis_size("rows")
    total = block_rows * owners
    index = lax.axis_index("rows") * block_rows + jnp.arange(block_rows, dtype=jnp.int32)
    offset = jnp.mod(cols - index[:, None] + HB, total) - HB
    offset = jnp.where(even, -offset, offset) + HB
    live = jnp.arange(slots, dtype=jnp.int32)[None, :] < counts[:, None]
    place = jnp.where(live, offset, DEAD)
    place = jnp.where(even, place[::-1], place)
    place = jnp.pad(place, ((0, 0), (0, 8 - slots)), constant_values=DEAD)
    table = jnp.broadcast_to(
        place.reshape(block_rows * 8, 1).astype(jnp.bfloat16), (block_rows * 8, 2 * tile)
    )
    paired = blocks.reshape(block_rows, 2, 2, tile, tile).transpose(0, 1, 3, 2, 4)
    paired = jnp.where(even, paired[::-1], paired)
    return jnp.concatenate([paired.reshape(block_rows * 2 * tile, 2 * tile), table], axis=0)


def body(start, blocks, cols, counts):
    tile = blocks.shape[3]
    rows_here = start.shape[1]
    columns = start.shape[2]
    owners = lax.axis_size("rows")
    sections = lax.axis_size("phase")
    even = lax.axis_index("rows") % 2 == 0
    first_core = lax.axis_index("phase") % 2 == 0
    to_a = [(i, i ^ 1) for i in range(owners)]
    to_b = [(i, (i + 1) % owners if i % 2 else (i - 1) % owners) for i in range(owners)]
    back = [(i, (i - 2) % sections) for i in range(sections)]
    mates = [(i, i ^ 1) for i in range(sections)]

    def mirrored(rows):
        tiles = rows.reshape(rows_here // tile, tile, columns)
        return jnp.where(even, tiles[::-1], tiles).reshape(rows_here, columns)

    travel = mirrored(start[0])
    home = packed_operator(blocks[0], cols[0], counts[0], even)
    here, ahead = home, lax.ppermute(home, "phase", back)
    ops = rows_here * 2
    visits = sections // 2
    for turn in range(visits):
        travel, here, ahead = lax.optimization_barrier((travel, here, ahead))
        later = lax.ppermute(ahead, "phase", back) if turn + 2 < visits else home
        a_side = jnp.concatenate([travel[:HALF], here[: 4 * tile], here[ops : ops + 16]], axis=0)
        b_side = jnp.concatenate([travel[HALF:], here[ops - 4 * tile : ops], here[ops + 48 :]], axis=0)
        from_a = lax.ppermute(a_side, "rows", to_a)
        from_b = lax.ppermute(b_side, "rows", to_b)
        other = lax.ppermute(jnp.where(first_core, ahead, here), "phase", mates)
        travel = visit(travel, from_a, from_b, here, other)
        here, ahead = ahead, later

    arrived = mirrored(travel)
    gram_term = lax.dot_general(
        arrived, arrived, (((0,), (0,)), ((), ())), preferred_element_type=jnp.float32
    )
    gram_total = sum_over_rows(gram_term.astype(jnp.bfloat16)) / (rows_here * owners)
    basis_out, upper_factor = finish(gram_total, arrived)
    return (basis_out[None], upper_factor[None])


def solution(mesh):
    placed = (
        P("phase", "rows", None),
        P("phase", "rows", None, None, None),
        P("phase", "rows", None),
        P("phase", "rows"),
    )
    return jax.shard_map(
        body,
        mesh=mesh,
        in_specs=placed,
        out_specs=(P("phase", "rows", None), P("phase", None, None)),
        check_vma=False,
    )
```

```python
import jax
import jax.numpy as jnp
from jax import lax
from jax.experimental import pallas as pl
from jax.experimental.pallas import tpu as pltpu
from jax.sharding import PartitionSpec as P


HB = 2
TILE = 128
HALF = 4 * TILE
DEAD = 7


def visit_kernel(cur, ra, rb, rim_a, rim_b, first, second, out, wide, mid):
    for n in range(4):
        wide[(3 - n) * TILE : (4 - n) * TILE, :] = ra[n * TILE : (n + 1) * TILE, :]
        wide[(15 - n) * TILE : (16 - n) * TILE, :] = rb[n * TILE : (n + 1) * TILE, :]
    wide[4 * TILE : 12 * TILE, :] = cur[...]
    zero = jnp.zeros((TILE, cur.shape[1]), cur.dtype)
    wide[16 * TILE :, :] = zero
    mid[12 * TILE :, :] = zero

    def row(ops, n, source, centre, sign, nothing):
        line = ops.shape[0] // (4 * TILE + 8) * 4 * TILE + n * 8
        table = ops[line : line + 8, :].astype(jnp.float32).astype(jnp.int32)

        def block(j):
            if j == 0:
                return source[centre * TILE : (centre + 1) * TILE, :]
            value = jnp.max(table[j : j + 1, :])
            place = jnp.where(value == DEAD, nothing, centre + sign * (value - 2))
            return source[pl.ds(pl.multiple_of(place * TILE, TILE), TILE), :]

        def slot(j):
            return ops[(n * 4 + j) * TILE : (n * 4 + j + 1) * TILE, :]

        total = None
        for j in (0, 2):
            left = jnp.concatenate([slot(j), slot(j + 1)], axis=1)
            right = jnp.concatenate([block(j), block(j + 1)], axis=0)
            part = jnp.dot(left, right, preferred_element_type=jnp.float32)
            total = part if total is None else total + part
        return total.astype(out.dtype)

    for n in range(2):
        c = 1 - n
        mid[c * TILE : (c + 1) * TILE, :] = row(rim_a, n, wide, c + 2, -1, 16)
        c = 11 - n
        mid[c * TILE : (c + 1) * TILE, :] = row(rim_b, n, wide, c + 2, -1, 16)
    for c in range(8):
        mid[(c + 2) * TILE : (c + 3) * TILE, :] = row(first, c, wide, c + 4, 1, 16)
    for c in range(8):
        out[c * TILE : (c + 1) * TILE, :] = row(second, c, mid, c + 2, 1, 12)


def visit(cur, ra, rb, rim_a, rim_b, first, second):
    vmem = pl.BlockSpec(memory_space=pltpu.VMEM)
    columns = cur.shape[1]
    return pl.pallas_call(
        visit_kernel,
        out_shape=jax.ShapeDtypeStruct(cur.shape, cur.dtype),
        in_specs=[vmem] * 7,
        out_specs=vmem,
        scratch_shapes=[
            pltpu.VMEM((17 * TILE, columns), cur.dtype),
            pltpu.VMEM((13 * TILE, columns), cur.dtype),
        ],
        compiler_params=pltpu.CompilerParams(vmem_limit_bytes=24 * 1024 * 1024),
        cost_estimate=pl.CostEstimate(flops=700_000_000, bytes_accessed=4_000_000, transcendentals=0),
        name="two_steps",
    )(cur, ra, rb, rim_a, rim_b, first, second)


NB = 16


def factor_kernel(gram_ref, arrived_ref, basis_ref, factor_ref, a_ref, w_ref):
    size = gram_ref.shape[0]
    a_ref[...] = gram_ref[...]
    row_i = lax.broadcasted_iota(jnp.int32, (size, size), 0)
    col_i = lax.broadcasted_iota(jnp.int32, (size, size), 1)
    w_ref[...] = jnp.where(row_i == col_i, 1.0, 0.0)
    lanes = 128
    sub = lax.broadcasted_iota(jnp.int32, (NB, lanes), 0)
    wide_row = lax.broadcasted_iota(jnp.int32, (NB, size), 0)
    wide_col = lax.broadcasted_iota(jnp.int32, (NB, size), 1)
    for first in range(0, size, NB):
        panel = a_ref[first : first + NB, :]
        other = w_ref[first : first + NB, :]
        columns = [
            jnp.broadcast_to(panel[:, first + k : first + k + 1], (NB, lanes))
            for k in range(NB)
        ]
        pivots = jnp.zeros((NB, lanes), jnp.float32)
        for j in range(NB):
            column = columns[j]
            pivot = jnp.broadcast_to(column[j : j + 1, :], (NB, lanes))
            pivots = jnp.where(sub == j, pivot, pivots)
            if j == NB - 1:
                break
            scaled = jnp.where(sub > j, column / pivot, 0.0)
            for k in range(j + 1, NB):
                columns[k] = columns[k] - scaled * jnp.broadcast_to(
                    column[k : k + 1, :], (NB, lanes)
                )
            both = jnp.concatenate([scaled] * (size // lanes), axis=1)
            panel = panel - both * jnp.broadcast_to(panel[j : j + 1, :], (NB, size))
            other = other - both * jnp.broadcast_to(other[j : j + 1, :], (NB, size))
        scale = 1.0 / jnp.sqrt(pivots)
        both = jnp.concatenate([scale] * (size // lanes), axis=1)
        upper = jnp.where(wide_col >= wide_row + first, panel * both, 0.0)
        other = other * both
        factor_ref[first : first + NB, :] = upper
        w_ref[first : first + NB, :] = other
        rest = first + NB
        if rest < size:
            low_row = rest // lanes * lanes
            low_lane = first // lanes * lanes
            high_lane = low_lane + lanes
            right = jnp.concatenate([upper[:, low_lane:], other[:, :high_lane]], axis=1)
            change = lax.dot_general(
                upper[:, low_row:], right, (((0,), (0,)), ((), ())),
                preferred_element_type=jnp.float32, precision=lax.Precision.HIGHEST,
            )[rest - low_row :, :]
            split = size - low_lane
            a_ref[rest:, low_lane:] = a_ref[rest:, low_lane:] - change[:, :split]
            w_ref[rest:, :high_lane] = w_ref[rest:, :high_lane] - change[:, split:]
    w = w_ref[...]
    high = w.astype(jnp.bfloat16)
    low = (w - high.astype(jnp.float32)).astype(jnp.bfloat16)
    dims = (((1,), (1,)), ((), ()))

    @pl.loop(0, arrived_ref.shape[0], step=256)
    def _(piece):
        at = pl.ds(pl.multiple_of(piece, 256), 256)
        rows = arrived_ref[at, :]
        basis_ref[at, :] = lax.dot_general(
            rows, high, dims, preferred_element_type=jnp.float32
        ) + lax.dot_general(rows, low, dims, preferred_element_type=jnp.float32)


def finish(gram, arrived):
    size = gram.shape[0]
    vmem = pl.BlockSpec(memory_space=pltpu.VMEM)
    return pl.pallas_call(
        factor_kernel,
        out_shape=(
            jax.ShapeDtypeStruct(arrived.shape, jnp.float32),
            jax.ShapeDtypeStruct((size, size), jnp.float32),
        ),
        in_specs=[vmem, vmem],
        out_specs=(vmem, vmem),
        scratch_shapes=[pltpu.VMEM((size, size), jnp.float32), pltpu.VMEM((size, size), jnp.float32)],
        name="factor_solve",
    )(gram, arrived)


def sum_over_rows(term):
    owners = lax.axis_size("rows")
    size = term.shape[0]
    pieces = term.reshape(owners, size // owners, size)
    pieces = lax.all_to_all(pieces, "rows", 0, 0, tiled=True)
    mine = jnp.sum(pieces.astype(jnp.float32), axis=0, keepdims=True)
    copies = jnp.broadcast_to(mine, (owners, size // owners, size))
    return lax.all_to_all(copies, "rows", 0, 0, tiled=True).reshape(size, size)


def packed_operator(blocks, cols, counts, even):
    block_rows, slots, tile, _ = blocks.shape
    owners = lax.axis_size("rows")
    total = block_rows * owners
    index = lax.axis_index("rows") * block_rows + jnp.arange(block_rows, dtype=jnp.int32)
    offset = jnp.mod(cols - index[:, None] + HB, total) - HB
    offset = jnp.where(even, -offset, offset) + HB
    live = jnp.arange(slots, dtype=jnp.int32)[None, :] < counts[:, None]
    place = jnp.where(live, offset, DEAD)
    place = jnp.where(even, place[::-1], place)
    place = jnp.pad(place, ((0, 0), (0, 8 - slots)), constant_values=DEAD)
    table = jnp.broadcast_to(
        place.reshape(block_rows * 8, 1).astype(jnp.bfloat16), (block_rows * 8, tile)
    )
    blocks = jnp.where(even, blocks[::-1], blocks)
    return jnp.concatenate([blocks.reshape(block_rows * slots * tile, tile), table], axis=0)


def body(start, blocks, cols, counts):
    block_rows, slots, tile = blocks.shape[1:4]
    rows_here = start.shape[1]
    columns = start.shape[2]
    owners = lax.axis_size("rows")
    sections = lax.axis_size("phase")
    even = lax.axis_index("rows") % 2 == 0
    first_core = lax.axis_index("phase") % 2 == 0
    to_a = [(i, i ^ 1) for i in range(owners)]
    to_b = [(i, (i + 1) % owners if i % 2 else (i - 1) % owners) for i in range(owners)]
    back = [(i, (i - 2) % sections) for i in range(sections)]
    ahead = [(i, (i + 2) % sections) for i in range(sections)]
    mates = [(i, i ^ 1) for i in range(sections)]
    lines = block_rows * slots * tile
    edge = HB * slots * tile

    def mirrored(rows):
        tiles = rows.reshape(rows_here // tile, tile, columns)
        return jnp.where(even, tiles[::-1], tiles).reshape(rows_here, columns)

    def rims(operator):
        a_side = jnp.concatenate([operator[:edge], operator[lines : lines + 8 * HB]], axis=0)
        b_side = jnp.concatenate([operator[lines - edge : lines], operator[-8 * HB :]], axis=0)
        return (lax.ppermute(a_side, "rows", to_a), lax.ppermute(b_side, "rows", to_b))

    visits = sections // 2
    far = visits // 2
    home = packed_operator(blocks[0], cols[0], counts[0], even)
    held = {0: home, visits: home}
    held[1] = lax.ppermute(home, "phase", back)
    held[visits - 1] = lax.ppermute(home, "phase", ahead)
    travel = mirrored(start[0])
    rim = rims(home)
    for turn in range(visits):
        from_a = lax.ppermute(travel[:HALF], "rows", to_a)
        from_b = lax.ppermute(travel[HALF:], "rows", to_b)
        here, later, travel = lax.optimization_barrier((held[turn], held[turn + 1], travel))
        if turn + 2 <= far:
            held[turn + 2] = lax.ppermute(later, "phase", back)
        end = visits - 1 - turn
        if turn > 0 and end > far:
            nearer, travel = lax.optimization_barrier((held[end + 1], travel))
            held[end] = lax.ppermute(nearer, "phase", ahead)
        other = lax.ppermute(jnp.where(first_core, later, here), "phase", mates)
        next_rim = rims(later) if turn + 1 < visits else None
        travel = visit(travel, from_a, from_b, *rim, here, other)
        rim = next_rim

    arrived = mirrored(travel)
    gram_term = lax.dot_general(
        arrived, arrived, (((0,), (0,)), ((), ())), preferred_element_type=jnp.float32
    )
    gram_total = sum_over_rows(gram_term.astype(jnp.bfloat16)) / (rows_here * owners)
    basis_out, upper_factor = finish(gram_total, arrived)
    return (basis_out[None], upper_factor[None])


def solution(mesh):
    placed = (
        P("phase", "rows", None),
        P("phase", "rows", None, None, None),
        P("phase", "rows", None),
        P("phase", "rows"),
    )
    return jax.shard_map(
        body,
        mesh=mesh,
        in_specs=placed,
        out_specs=(P("phase", "rows", None), P("phase", None, None)),
        check_vma=False,
    )
```

```python
import functools

import jax
import jax.numpy as jnp
from jax import lax
from jax.experimental import pallas as pl
from jax.experimental.pallas import tpu as pltpu
from jax.sharding import PartitionSpec as P


HB = 2
TILE = 128
HALF = 4 * TILE
DEAD = 7

def visit_kernel(cur_a, cur_b, ra, rb, rim_a, rim_b, first, second, out_a, out_b, wide, mid):
    for n in range(4):
        wide[(3 - n) * TILE : (4 - n) * TILE, :] = ra[n * TILE : (n + 1) * TILE, :]
        wide[(15 - n) * TILE : (16 - n) * TILE, :] = rb[n * TILE : (n + 1) * TILE, :]
    wide[4 * TILE : 8 * TILE, :] = cur_a[...]
    wide[8 * TILE : 12 * TILE, :] = cur_b[...]
    zero = jnp.zeros((TILE, cur_a.shape[1]), cur_a.dtype)
    wide[16 * TILE :, :] = zero
    mid[12 * TILE :, :] = zero

    def row(ops, n, source, centre, sign, nothing):
        line = ops.shape[0] // (4 * TILE + 8) * 4 * TILE + n * 8
        table = ops[line : line + 8, :].astype(jnp.float32).astype(jnp.int32)

        def block(j):
            if j == 0:
                return source[centre * TILE : (centre + 1) * TILE, :]
            value = jnp.max(table[j : j + 1, :])
            place = jnp.where(value == DEAD, nothing, centre + sign * (value - 2))
            return source[pl.ds(pl.multiple_of(place * TILE, TILE), TILE), :]

        def slot(j):
            return ops[(n * 4 + j) * TILE : (n * 4 + j + 1) * TILE, :]

        total = None
        for j in (0, 2):
            left = jnp.concatenate([slot(j), slot(j + 1)], axis=1)
            right = jnp.concatenate([block(j), block(j + 1)], axis=0)
            part = jnp.dot(left, right, preferred_element_type=jnp.float32)
            total = part if total is None else total + part
        return total.astype(out_a.dtype)

    for n in range(2):
        c = 1 - n
        mid[c * TILE : (c + 1) * TILE, :] = row(rim_a, n, wide, c + 2, -1, 16)
        c = 11 - n
        mid[c * TILE : (c + 1) * TILE, :] = row(rim_b, n, wide, c + 2, -1, 16)
    for c in range(8):
        mid[(c + 2) * TILE : (c + 3) * TILE, :] = row(first, c, wide, c + 4, 1, 16)
    for c in range(8):
        half = out_a if c < 4 else out_b
        half[c % 4 * TILE : (c % 4 + 1) * TILE, :] = row(second, c, mid, c + 2, 1, 12)

def visit(halves, ra, rb, rim_a, rim_b, first, second):
    vmem = pl.BlockSpec(memory_space=pltpu.VMEM)
    shape = jax.ShapeDtypeStruct(halves[0].shape, halves[0].dtype)
    columns = shape.shape[1]
    return pl.pallas_call(
        visit_kernel,
        out_shape=(shape, shape),
        in_specs=[vmem] * 8,
        out_specs=(vmem, vmem),
        scratch_shapes=[
            pltpu.VMEM((17 * TILE, columns), shape.dtype),
            pltpu.VMEM((13 * TILE, columns), shape.dtype),
        ],
        compiler_params=pltpu.CompilerParams(vmem_limit_bytes=24 * 1024 * 1024),
        cost_estimate=pl.CostEstimate(flops=700_000_000, bytes_accessed=4_000_000, transcendentals=0),
        name="two_steps",
    )(*halves, ra, rb, rim_a, rim_b, first, second)

def pack_kernel(total, info, cols, counts, blocks, packed, rim_a, rim_b):
    even = info[0]
    block_rows, slots = cols.shape
    span = slots * TILE
    lines = block_rows * span
    line = lax.broadcasted_iota(jnp.int32, (8, TILE), 0)
    for c in range(0, block_rows, 2):
        tables = []
        for i in range(2):
            source = jnp.where(even == 1, block_rows - 1 - (c + i), c + i)
            packed[(c + i) * span : (c + i + 1) * span, :] = blocks[
                pl.ds(pl.multiple_of(source * span, span), span), :
            ]
            table = jnp.full((8, TILE), DEAD, jnp.int32)
            for j in range(slots):
                offset = lax.rem(cols[source, j] - info[1] - source + HB + total, total)
                offset = jnp.where(even == 1, 2 * HB - offset, offset)
                value = jnp.where(j < counts[source], offset, DEAD)
                table = jnp.where(line == j, value, table)
            tables.append(table.astype(jnp.float32))
        both = jnp.concatenate(tables, axis=0).astype(packed.dtype)
        packed[lines + c * 8 : lines + c * 8 + 16, :] = both
    edge = HB * span
    rim_a[:edge, :] = packed[:edge, :]
    rim_a[edge:, :] = packed[lines : lines + 8 * HB, :]
    rim_b[:edge, :] = packed[lines - edge : lines, :]
    rim_b[edge:, :] = packed[lines + 8 * (block_rows - HB) :, :]

def pack(total, info, cols, counts, blocks):
    block_rows, slots, tile, _ = blocks.shape
    lines = block_rows * slots * tile
    vmem = pl.BlockSpec(memory_space=pltpu.VMEM)
    smem = pl.BlockSpec(memory_space=pltpu.SMEM)
    rim = jax.ShapeDtypeStruct((HB * slots * tile + 8 * HB, tile), blocks.dtype)
    whole = jax.ShapeDtypeStruct((lines + 8 * block_rows, tile), blocks.dtype)
    return pl.pallas_call(
        functools.partial(pack_kernel, total),
        out_shape=(whole, rim, rim),
        in_specs=[smem, smem, smem, vmem],
        out_specs=(vmem, vmem, vmem),
        compiler_params=pltpu.CompilerParams(vmem_limit_bytes=16 * 1024 * 1024),
        name="pack_operator",
    )(info, cols, counts, blocks.reshape(lines, tile))

def halve_kernel(info, start, half_a, half_b):
    block_rows = start.shape[0] // TILE
    for c in range(block_rows):
        source = jnp.where(info[0] == 1, block_rows - 1 - c, c)
        half = half_a if c < 4 else half_b
        half[c % 4 * TILE : (c % 4 + 1) * TILE, :] = start[
            pl.ds(pl.multiple_of(source * TILE, TILE), TILE), :
        ]

def halve(info, start):
    vmem = pl.BlockSpec(memory_space=pltpu.VMEM)
    half = jax.ShapeDtypeStruct((HALF, start.shape[1]), start.dtype)
    return pl.pallas_call(
        halve_kernel,
        out_shape=(half, half),
        in_specs=[pl.BlockSpec(memory_space=pltpu.SMEM), vmem],
        out_specs=(vmem, vmem),
        compiler_params=pltpu.CompilerParams(vmem_limit_bytes=8 * 1024 * 1024),
        name="halve_start",
    )(info, start)


NB = 16

def factor_kernel(info, gram_ref, half_a, half_b, basis_ref, factor_ref, a_ref, w_ref):
    size = gram_ref.shape[0]
    a_ref[...] = gram_ref[...]
    row_i = lax.broadcasted_iota(jnp.int32, (size, size), 0)
    col_i = lax.broadcasted_iota(jnp.int32, (size, size), 1)
    w_ref[...] = jnp.where(row_i == col_i, 1.0, 0.0)
    lanes = 128
    sub = lax.broadcasted_iota(jnp.int32, (NB, lanes), 0)
    wide_row = lax.broadcasted_iota(jnp.int32, (NB, size), 0)
    wide_col = lax.broadcasted_iota(jnp.int32, (NB, size), 1)
    for first in range(0, size, NB):
        panel = a_ref[first : first + NB, :]
        other = w_ref[first : first + NB, :]
        columns = [
            jnp.broadcast_to(panel[:, first + k : first + k + 1], (NB, lanes))
            for k in range(NB)
        ]
        pivots = jnp.zeros((NB, lanes), jnp.float32)
        for j in range(NB):
            column = columns[j]
            pivot = jnp.broadcast_to(column[j : j + 1, :], (NB, lanes))
            pivots = jnp.where(sub == j, pivot, pivots)
            if j == NB - 1:
                break
            scaled = jnp.where(sub > j, column / pivot, 0.0)
            for k in range(j + 1, NB):
                columns[k] = columns[k] - scaled * jnp.broadcast_to(
                    column[k : k + 1, :], (NB, lanes)
                )
            both = jnp.concatenate([scaled] * (size // lanes), axis=1)
            panel = panel - both * jnp.broadcast_to(panel[j : j + 1, :], (NB, size))
            other = other - both * jnp.broadcast_to(other[j : j + 1, :], (NB, size))
        scale = 1.0 / jnp.sqrt(pivots)
        both = jnp.concatenate([scale] * (size // lanes), axis=1)
        upper = jnp.where(wide_col >= wide_row + first, panel * both, 0.0)
        other = other * both
        factor_ref[first : first + NB, :] = upper
        w_ref[first : first + NB, :] = other
        rest = first + NB
        if rest < size:
            low_row = rest // lanes * lanes
            low_lane = first // lanes * lanes
            high_lane = low_lane + lanes
            right = jnp.concatenate([upper[:, low_lane:], other[:, :high_lane]], axis=1)
            change = lax.dot_general(
                upper[:, low_row:], right, (((0,), (0,)), ((), ())),
                preferred_element_type=jnp.float32, precision=lax.Precision.HIGHEST,
            )[rest - low_row :, :]
            split = size - low_lane
            a_ref[rest:, low_lane:] = a_ref[rest:, low_lane:] - change[:, :split]
            w_ref[rest:, :high_lane] = w_ref[rest:, :high_lane] - change[:, split:]
    w = w_ref[...]
    high = w.astype(jnp.bfloat16)
    low = (w - high.astype(jnp.float32)).astype(jnp.bfloat16)
    dims = (((1,), (1,)), ((), ()))
    for c in range(8):
        half = half_a if c < 4 else half_b
        rows = half[c % 4 * TILE : (c % 4 + 1) * TILE, :]
        place = jnp.where(info[0] == 1, 7 - c, c)
        basis_ref[pl.ds(pl.multiple_of(place * TILE, TILE), TILE), :] = lax.dot_general(
            rows, high, dims, preferred_element_type=jnp.float32
        ) + lax.dot_general(rows, low, dims, preferred_element_type=jnp.float32)

def finish(info, gram, halves):
    size = gram.shape[0]
    vmem = pl.BlockSpec(memory_space=pltpu.VMEM)
    return pl.pallas_call(
        factor_kernel,
        out_shape=(
            jax.ShapeDtypeStruct((2 * HALF, size), jnp.float32),
            jax.ShapeDtypeStruct((size, size), jnp.float32),
        ),
        in_specs=[pl.BlockSpec(memory_space=pltpu.SMEM), vmem, vmem, vmem],
        out_specs=(vmem, vmem),
        scratch_shapes=[pltpu.VMEM((size, size), jnp.float32), pltpu.VMEM((size, size), jnp.float32)],
        name="factor_solve",
    )(info, gram, *halves)


def sum_over_rows(term):
    owners = lax.axis_size("rows")
    size = term.shape[0]
    pieces = term.reshape(owners, size // owners, size)
    pieces = lax.all_to_all(pieces, "rows", 0, 0, tiled=True)
    mine = jnp.sum(pieces.astype(jnp.float32), axis=0, keepdims=True)
    copies = jnp.broadcast_to(mine, (owners, size // owners, size))
    return lax.all_to_all(copies, "rows", 0, 0, tiled=True).reshape(size, size)


def body(start, blocks, cols, counts):
    block_rows, slots, tile = blocks.shape[1:4]
    rows_here = start.shape[1]
    owners = lax.axis_size("rows")
    sections = lax.axis_size("phase")
    place = lax.axis_index("rows")
    info = jnp.stack([1 - place % 2, place * block_rows]).astype(jnp.int32)
    first_core = lax.axis_index("phase") % 2 == 0
    to_a = [(i, i ^ 1) for i in range(owners)]
    to_b = [(i, (i + 1) % owners if i % 2 else (i - 1) % owners) for i in range(owners)]
    back = [(i, (i - 2) % sections) for i in range(sections)]
    ahead = [(i, (i + 2) % sections) for i in range(sections)]
    mates = [(i, i ^ 1) for i in range(sections)]
    lines = block_rows * slots * tile
    edge = HB * slots * tile

    def rims(a_side, b_side):
        return (lax.ppermute(a_side, "rows", to_a), lax.ppermute(b_side, "rows", to_b))

    def rims_of(operator):
        a_side = jnp.concatenate([operator[:edge], operator[lines : lines + 8 * HB]], axis=0)
        b_side = jnp.concatenate([operator[lines - edge : lines], operator[-8 * HB :]], axis=0)
        return a_side, b_side

    visits = sections // 2
    far = visits // 2
    home, home_a, home_b = pack(block_rows * owners, info, cols[0], counts[0], blocks[0])
    held = {0: home, visits: home}
    held[1] = lax.ppermute(home, "phase", back)
    held[visits - 1] = lax.ppermute(home, "phase", ahead)
    halves = halve(info, start[0])
    rim = rims(home_a, home_b)
    for turn in range(visits):
        from_a = lax.ppermute(halves[0], "rows", to_a)
        from_b = lax.ppermute(halves[1], "rows", to_b)
        here, later = held[turn], held[turn + 1]
        if 0 < turn < far:
            here, later, from_a, from_b = lax.optimization_barrier((here, later, from_a, from_b))
        else:
            here, later, halves = lax.optimization_barrier((here, later, halves))
        if turn + 2 <= far:
            held[turn + 2] = lax.ppermute(later, "phase", back)
        end = visits - 1 - turn
        if turn > 0 and end > far:
            nearer, from_a = lax.optimization_barrier((held[end + 1], from_a))
            held[end] = lax.ppermute(nearer, "phase", ahead)
        other = lax.ppermute(jnp.where(first_core, later, here), "phase", mates)
        next_rim = rims(*rims_of(later)) if turn + 1 < visits else None
        halves = visit(halves, from_a, from_b, *rim, here, other)
        rim = next_rim

    arrived = jnp.concatenate(halves, axis=0)
    gram_term = lax.dot_general(
        arrived, arrived, (((0,), (0,)), ((), ())), preferred_element_type=jnp.float32
    )
    gram_total = sum_over_rows(gram_term.astype(jnp.bfloat16)) / (rows_here * owners)
    basis_out, upper_factor = finish(info, gram_total, halves)
    return (basis_out[None], upper_factor[None])


def solution(mesh):
    placed = (
        P("phase", "rows", None),
        P("phase", "rows", None, None, None),
        P("phase", "rows", None),
        P("phase", "rows"),
    )
    return jax.shard_map(
        body,
        mesh=mesh,
        in_specs=placed,
        out_specs=(P("phase", "rows", None), P("phase", None, None)),
        check_vma=False,
    )
```

```python
import functools

import jax
import jax.numpy as jnp
from jax import lax
from jax.experimental import pallas as pl
from jax.experimental.pallas import tpu as pltpu
from jax.sharding import PartitionSpec as P


HB = 2
TILE = 128
HALF = 4 * TILE
DEAD = 7

def visit_kernel(rim_at, second_at, cur_a, cur_b, ra, rb, rim_a, rim_b, first, second, out_a, out_b, wide, mid):
    for n in range(4):
        wide[(3 - n) * TILE : (4 - n) * TILE, :] = ra[n * TILE : (n + 1) * TILE, :]
        wide[(15 - n) * TILE : (16 - n) * TILE, :] = rb[n * TILE : (n + 1) * TILE, :]
    wide[4 * TILE : 8 * TILE, :] = cur_a[...]
    wide[8 * TILE : 12 * TILE, :] = cur_b[...]
    zero = jnp.zeros((TILE, cur_a.shape[1]), cur_a.dtype)
    wide[16 * TILE :, :] = zero
    mid[12 * TILE :, :] = zero

    def row(ops, at, count, n, source, centre, sign, nothing):
        line = at + count * 4 * TILE + n * 8
        table = ops[line : line + 8, :].astype(jnp.float32).astype(jnp.int32)

        def block(j):
            if j == 0:
                return source[centre * TILE : (centre + 1) * TILE, :]
            value = jnp.max(table[j : j + 1, :])
            place = jnp.where(value == DEAD, nothing, centre + sign * (value - 2))
            return source[pl.ds(pl.multiple_of(place * TILE, TILE), TILE), :]

        def slot(j):
            return ops[at + (n * 4 + j) * TILE : at + (n * 4 + j + 1) * TILE, :]

        total = None
        for j in (0, 2):
            left = jnp.concatenate([slot(j), slot(j + 1)], axis=1)
            right = jnp.concatenate([block(j), block(j + 1)], axis=0)
            part = jnp.dot(left, right, preferred_element_type=jnp.float32)
            total = part if total is None else total + part
        return total.astype(out_a.dtype)

    for n in range(2):
        c = 1 - n
        mid[c * TILE : (c + 1) * TILE, :] = row(rim_a, rim_at, 2, n, wide, c + 2, -1, 16)
        c = 11 - n
        mid[c * TILE : (c + 1) * TILE, :] = row(rim_b, rim_at, 2, n, wide, c + 2, -1, 16)
    for c in range(8):
        mid[(c + 2) * TILE : (c + 3) * TILE, :] = row(first, 0, 8, c, wide, c + 4, 1, 16)
    for c in range(8):
        half = out_a if c < 4 else out_b
        half[c % 4 * TILE : (c % 4 + 1) * TILE, :] = row(second, second_at, 8, c, mid, c + 2, 1, 12)

def visit(halves, ra, rb, rim_a, rim_b, first, second, rim_at=0, second_at=0):
    vmem = pl.BlockSpec(memory_space=pltpu.VMEM)
    shape = jax.ShapeDtypeStruct(halves[0].shape, halves[0].dtype)
    columns = shape.shape[1]
    return pl.pallas_call(
        functools.partial(visit_kernel, rim_at, second_at),
        out_shape=(shape, shape),
        in_specs=[vmem] * 8,
        out_specs=(vmem, vmem),
        scratch_shapes=[
            pltpu.VMEM((17 * TILE, columns), shape.dtype),
            pltpu.VMEM((13 * TILE, columns), shape.dtype),
        ],
        compiler_params=pltpu.CompilerParams(vmem_limit_bytes=24 * 1024 * 1024),
        cost_estimate=pl.CostEstimate(flops=700_000_000, bytes_accessed=4_000_000, transcendentals=0),
        name="two_steps",
    )(*halves, ra, rb, rim_a, rim_b, first, second)

def pack_kernel(total, info, cols, counts, blocks, packed, rim_a, rim_b):
    even = info[0]
    block_rows, slots = cols.shape
    span = slots * TILE
    lines = block_rows * span
    line = lax.broadcasted_iota(jnp.int32, (8, TILE), 0)
    for c in range(0, block_rows, 2):
        tables = []
        for i in range(2):
            source = jnp.where(even == 1, block_rows - 1 - (c + i), c + i)
            packed[(c + i) * span : (c + i + 1) * span, :] = blocks[
                pl.ds(pl.multiple_of(source * span, span), span), :
            ]
            table = jnp.full((8, TILE), DEAD, jnp.int32)
            for j in range(slots):
                offset = lax.rem(cols[source, j] - info[1] - source + HB + total, total)
                offset = jnp.where(even == 1, 2 * HB - offset, offset)
                value = jnp.where(j < counts[source], offset, DEAD)
                table = jnp.where(line == j, value, table)
            tables.append(table.astype(jnp.float32))
        both = jnp.concatenate(tables, axis=0).astype(packed.dtype)
        packed[lines + c * 8 : lines + c * 8 + 16, :] = both
    edge = HB * span
    rim_a[:edge, :] = packed[:edge, :]
    rim_a[edge:, :] = packed[lines : lines + 8 * HB, :]
    rim_b[:edge, :] = packed[lines - edge : lines, :]
    rim_b[edge:, :] = packed[lines + 8 * (block_rows - HB) :, :]

def pack(total, info, cols, counts, blocks):
    block_rows, slots, tile, _ = blocks.shape
    lines = block_rows * slots * tile
    vmem = pl.BlockSpec(memory_space=pltpu.VMEM)
    smem = pl.BlockSpec(memory_space=pltpu.SMEM)
    rim = jax.ShapeDtypeStruct((HB * slots * tile + 8 * HB, tile), blocks.dtype)
    whole = jax.ShapeDtypeStruct((lines + 8 * block_rows, tile), blocks.dtype)
    return pl.pallas_call(
        functools.partial(pack_kernel, total),
        out_shape=(whole, rim, rim),
        in_specs=[smem, smem, smem, vmem],
        out_specs=(vmem, vmem, vmem),
        compiler_params=pltpu.CompilerParams(vmem_limit_bytes=16 * 1024 * 1024),
        name="pack_operator",
    )(info, cols, counts, blocks.reshape(lines, tile))

def halve_kernel(info, start, half_a, half_b):
    block_rows = start.shape[0] // TILE
    for c in range(block_rows):
        source = jnp.where(info[0] == 1, block_rows - 1 - c, c)
        half = half_a if c < 4 else half_b
        half[c % 4 * TILE : (c % 4 + 1) * TILE, :] = start[
            pl.ds(pl.multiple_of(source * TILE, TILE), TILE), :
        ]

def halve(info, start):
    vmem = pl.BlockSpec(memory_space=pltpu.VMEM)
    half = jax.ShapeDtypeStruct((HALF, start.shape[1]), start.dtype)
    return pl.pallas_call(
        halve_kernel,
        out_shape=(half, half),
        in_specs=[pl.BlockSpec(memory_space=pltpu.SMEM), vmem],
        out_specs=(vmem, vmem),
        compiler_params=pltpu.CompilerParams(vmem_limit_bytes=8 * 1024 * 1024),
        name="halve_start",
    )(info, start)

def gather_kernel(info, *refs):
    operators, (side_a, side_b, swapped) = refs[:-3], refs[-3:]
    span = operators[0].shape[0]
    rim = side_a.shape[0] // (len(operators) - 1)
    tables = 8 * HB

    for n, (operator, following) in enumerate(zip(operators[:-1], operators[1:])):
        @pl.loop(0, span, step=160)
        def _(line):
            at = pl.ds(pl.multiple_of(line, 32), 160)
            to = pl.ds(pl.multiple_of(n * span + line, 32), 160)
            swapped[to, :] = jnp.where(info[2] == 0, following[at, :], operator[at, :])

        edge = rim - tables
        body = span - span // (4 * TILE + 8) * 8

        @pl.loop(0, edge, step=TILE)
        def _(line):
            at = pl.multiple_of(line, TILE)
            to = pl.ds(pl.multiple_of(n * rim + line, 16), TILE)
            side_a[to, :] = operator[pl.ds(at, TILE), :]
            side_b[to, :] = operator[pl.ds(body - edge + at, TILE), :]

        at = n * rim + edge
        side_a[at : at + tables, :] = operator[body : body + tables, :]
        side_b[at : at + tables, :] = operator[span - tables :, :]

def gather_last(info, rim_rows, operators):
    vmem = pl.BlockSpec(memory_space=pltpu.VMEM)
    kind = operators[0].dtype
    count = len(operators) - 1
    side = jax.ShapeDtypeStruct((count * rim_rows, TILE), kind)
    swapped = jax.ShapeDtypeStruct((count * operators[0].shape[0], TILE), kind)
    return pl.pallas_call(
        gather_kernel,
        out_shape=(side, side, swapped),
        in_specs=[pl.BlockSpec(memory_space=pltpu.SMEM)] + [vmem] * len(operators),
        out_specs=(vmem, vmem, vmem),
        compiler_params=pltpu.CompilerParams(vmem_limit_bytes=24 * 1024 * 1024),
        name="gather_last",
    )(info, *operators)


NB = 16

def factor_kernel(info, gram_ref, half_a, half_b, basis_ref, factor_ref, a_ref, w_ref):
    size = gram_ref.shape[0]
    a_ref[...] = gram_ref[...]
    row_i = lax.broadcasted_iota(jnp.int32, (size, size), 0)
    col_i = lax.broadcasted_iota(jnp.int32, (size, size), 1)
    w_ref[...] = jnp.where(row_i == col_i, 1.0, 0.0)
    lanes = 128
    sub = lax.broadcasted_iota(jnp.int32, (NB, lanes), 0)
    wide_row = lax.broadcasted_iota(jnp.int32, (NB, size), 0)
    wide_col = lax.broadcasted_iota(jnp.int32, (NB, size), 1)
    for first in range(0, size, NB):
        panel = a_ref[first : first + NB, :]
        other = w_ref[first : first + NB, :]
        columns = [
            jnp.broadcast_to(panel[:, first + k : first + k + 1], (NB, lanes))
            for k in range(NB)
        ]
        pivots = jnp.zeros((NB, lanes), jnp.float32)
        for j in range(NB):
            column = columns[j]
            pivot = jnp.broadcast_to(column[j : j + 1, :], (NB, lanes))
            pivots = jnp.where(sub == j, pivot, pivots)
            if j == NB - 1:
                break
            scaled = jnp.where(sub > j, column / pivot, 0.0)
            for k in range(j + 1, NB):
                columns[k] = columns[k] - scaled * jnp.broadcast_to(
                    column[k : k + 1, :], (NB, lanes)
                )
            both = jnp.concatenate([scaled] * (size // lanes), axis=1)
            panel = panel - both * jnp.broadcast_to(panel[j : j + 1, :], (NB, size))
            other = other - both * jnp.broadcast_to(other[j : j + 1, :], (NB, size))
        scale = 1.0 / jnp.sqrt(pivots)
        both = jnp.concatenate([scale] * (size // lanes), axis=1)
        upper = jnp.where(wide_col >= wide_row + first, panel * both, 0.0)
        other = other * both
        factor_ref[first : first + NB, :] = upper
        w_ref[first : first + NB, :] = other
        rest = first + NB
        if rest < size:
            low_row = rest // lanes * lanes
            low_lane = first // lanes * lanes
            high_lane = low_lane + lanes
            right = jnp.concatenate([upper[:, low_lane:], other[:, :high_lane]], axis=1)
            change = lax.dot_general(
                upper[:, low_row:], right, (((0,), (0,)), ((), ())),
                preferred_element_type=jnp.float32, precision=lax.Precision.HIGHEST,
            )[rest - low_row :, :]
            split = size - low_lane
            a_ref[rest:, low_lane:] = a_ref[rest:, low_lane:] - change[:, :split]
            w_ref[rest:, :high_lane] = w_ref[rest:, :high_lane] - change[:, split:]
    w = w_ref[...]
    high = w.astype(jnp.bfloat16)
    low = (w - high.astype(jnp.float32)).astype(jnp.bfloat16)
    dims = (((1,), (1,)), ((), ()))
    for c in range(8):
        half = half_a if c < 4 else half_b
        rows = half[c % 4 * TILE : (c % 4 + 1) * TILE, :]
        place = jnp.where(info[0] == 1, 7 - c, c)
        basis_ref[pl.ds(pl.multiple_of(place * TILE, TILE), TILE), :] = lax.dot_general(
            rows, high, dims, preferred_element_type=jnp.float32
        ) + lax.dot_general(rows, low, dims, preferred_element_type=jnp.float32)

def finish(info, gram, halves):
    size = gram.shape[0]
    vmem = pl.BlockSpec(memory_space=pltpu.VMEM)
    return pl.pallas_call(
        factor_kernel,
        out_shape=(
            jax.ShapeDtypeStruct((2 * HALF, size), jnp.float32),
            jax.ShapeDtypeStruct((size, size), jnp.float32),
        ),
        in_specs=[pl.BlockSpec(memory_space=pltpu.SMEM), vmem, vmem, vmem],
        out_specs=(vmem, vmem),
        scratch_shapes=[pltpu.VMEM((size, size), jnp.float32), pltpu.VMEM((size, size), jnp.float32)],
        name="factor_solve",
    )(info, gram, *halves)


def sum_over_rows(term):
    owners = lax.axis_size("rows")
    size = term.shape[0]
    pieces = term.reshape(owners, size // owners, size)
    pieces = lax.all_to_all(pieces, "rows", 0, 0, tiled=True)
    mine = jnp.sum(pieces.astype(jnp.float32), axis=0, keepdims=True)
    copies = jnp.broadcast_to(mine, (owners, size // owners, size))
    return lax.all_to_all(copies, "rows", 0, 0, tiled=True).reshape(size, size)


def body(start, blocks, cols, counts):
    block_rows, slots, tile = blocks.shape[1:4]
    rows_here = start.shape[1]
    owners = lax.axis_size("rows")
    sections = lax.axis_size("phase")
    place = lax.axis_index("rows")
    core = lax.axis_index("phase") % 2
    info = jnp.stack([1 - place % 2, place * block_rows, core]).astype(jnp.int32)
    first_core = core == 0
    to_a = [(i, i ^ 1) for i in range(owners)]
    to_b = [(i, (i + 1) % owners if i % 2 else (i - 1) % owners) for i in range(owners)]
    back = [(i, (i - 2) % sections) for i in range(sections)]
    ahead = [(i, (i + 2) % sections) for i in range(sections)]
    mates = [(i, i ^ 1) for i in range(sections)]
    lines = block_rows * slots * tile
    edge = HB * slots * tile

    def rims(a_side, b_side):
        return (lax.ppermute(a_side, "rows", to_a), lax.ppermute(b_side, "rows", to_b))

    def rims_of(operator):
        a_side = jnp.concatenate([operator[:edge], operator[lines : lines + 8 * HB]], axis=0)
        b_side = jnp.concatenate([operator[lines - edge : lines], operator[-8 * HB :]], axis=0)
        return a_side, b_side

    visits = sections // 2
    far = visits // 2
    home, home_a, home_b = pack(block_rows * owners, info, cols[0], counts[0], blocks[0])
    held = {0: home, visits: home}
    held[1] = lax.ppermute(home, "phase", back)
    held[visits - 1] = lax.ppermute(home, "phase", ahead)
    halves = halve(info, start[0])
    rim = rims(home_a, home_b)
    span = home.shape[0]
    rim_span = home_a.shape[0]
    for turn in range(visits):
        from_a = lax.ppermute(halves[0], "rows", to_a)
        from_b = lax.ppermute(halves[1], "rows", to_b)
        if turn <= far:
            here, later, halves = lax.optimization_barrier((held[turn], held[turn + 1], halves))
            if turn + 2 <= far:
                held[turn + 2] = lax.ppermute(later, "phase", back)
            end = visits - 1 - turn
            if turn > 0 and end > far:
                nearer, halves = lax.optimization_barrier((held[end + 1], halves))
                held[end] = lax.ppermute(nearer, "phase", ahead)
            picked = jnp.where(first_core, later, here)
            other, other_at, rim_at = lax.ppermute(picked, "phase", mates), 0, 0
        if turn < far:
            next_rim = rims(*rims_of(later))
        elif turn == far:
            last = [later] + [held[n] for n in range(turn + 2, visits)] + [home]
            side_a, side_b, swapped = gather_last(info, rim_span, last)
            next_rim = rims(side_a, side_b)
            others = lax.ppermute(swapped, "phase", mates)
        else:
            other, other_at, rim_at = others, (turn - far - 1) * span, (turn - far - 1) * rim_span
        halves = visit(halves, from_a, from_b, *rim, held[turn], other, rim_at, other_at)
        if turn <= far:
            rim = next_rim

    arrived = jnp.concatenate(halves, axis=0)
    gram_term = lax.dot_general(
        arrived, arrived, (((0,), (0,)), ((), ())), preferred_element_type=jnp.float32
    )
    gram_total = sum_over_rows(gram_term.astype(jnp.bfloat16)) / (rows_here * owners)
    basis_out, upper_factor = finish(info, gram_total, halves)
    return (basis_out[None], upper_factor[None])


def solution(mesh):
    placed = (
        P("phase", "rows", None),
        P("phase", "rows", None, None, None),
        P("phase", "rows", None),
        P("phase", "rows"),
    )
    return jax.shard_map(
        body,
        mesh=mesh,
        in_specs=placed,
        out_specs=(P("phase", "rows", None), P("phase", None, None)),
        check_vma=False,
    )
```

```python
import functools

import jax
import jax.numpy as jnp
from jax import lax
from jax.experimental import pallas as pl
from jax.experimental.pallas import tpu as pltpu
from jax.sharding import PartitionSpec as P


HB = 2
TILE = 128
HALF = 4 * TILE
DEAD = 7

def copy_rims(operator, side_a, side_b, at):
    span = operator.shape[0]
    body = span - span // (4 * TILE + 8) * 8
    edge = HB * 4 * TILE
    tables = 8 * HB

    @pl.loop(0, edge, step=TILE)
    def _(line):
        line = pl.multiple_of(line, TILE)
        to = pl.ds(pl.multiple_of(at + line, 16), TILE)
        side_a[to, :] = operator[pl.ds(line, TILE), :]
        side_b[to, :] = operator[pl.ds(body - edge + line, TILE), :]

    at = at + edge
    side_a[at : at + tables, :] = operator[body : body + tables, :]
    side_b[at : at + tables, :] = operator[span - tables :, :]

def visit_kernel(rim_at, second_at, flat, *refs):
    cur_a, cur_b, ra, rb, rim_a, rim_b, first, second = refs[:8]
    out_a, out_b, wide, mid = refs[-4:]

    def pieces(ref, n):
        for part in range(2):
            at = part * HALF + n * TILE
            yield slice(part * TILE, (part + 1) * TILE), ref[at : at + TILE, :]

    for n in range(4):
        for place, ref in ((3 - n, ra), (15 - n, rb), (4 + n, cur_a), (8 + n, cur_b)):
            for lanes, piece in pieces(ref, n):
                wide[place * TILE : (place + 1) * TILE, lanes] = piece
    zero = jnp.zeros((TILE, 2 * TILE), wide.dtype)
    wide[16 * TILE :, :] = zero
    mid[12 * TILE :, :] = zero

    def row(ops, at, count, n, source, centre, sign, nothing):
        line = at + count * 4 * TILE + n * 8
        table = ops[line : line + 8, :].astype(jnp.float32).astype(jnp.int32)

        def block(j):
            if j == 0:
                return source[centre * TILE : (centre + 1) * TILE, :]
            value = jnp.max(table[j : j + 1, :])
            place = jnp.where(value == DEAD, nothing, centre + sign * (value - 2))
            return source[pl.ds(pl.multiple_of(place * TILE, TILE), TILE), :]

        def slot(j):
            return ops[at + (n * 4 + j) * TILE : at + (n * 4 + j + 1) * TILE, :]

        total = None
        for j in (0, 2):
            left = jnp.concatenate([slot(j), slot(j + 1)], axis=1)
            right = jnp.concatenate([block(j), block(j + 1)], axis=0)
            part = jnp.dot(left, right, preferred_element_type=jnp.float32)
            total = part if total is None else total + part
        return total.astype(out_a.dtype)

    for n in range(2):
        c = 1 - n
        mid[c * TILE : (c + 1) * TILE, :] = row(rim_a, rim_at, 2, n, wide, c + 2, -1, 16)
        c = 11 - n
        mid[c * TILE : (c + 1) * TILE, :] = row(rim_b, rim_at, 2, n, wide, c + 2, -1, 16)
    for c in range(8):
        mid[(c + 2) * TILE : (c + 3) * TILE, :] = row(first, 0, 8, c, wide, c + 4, 1, 16)
    for c in range(8):
        half = out_a if c < 4 else out_b
        value = row(second, second_at, 8, c, mid, c + 2, 1, 12)
        at = c % 4 * TILE
        if flat:
            half[at : at + TILE, :] = value
        else:
            half[at : at + TILE, :] = value[:, :TILE]
            half[HALF + at : HALF + at + TILE, :] = value[:, TILE:]
    if len(refs) == 13:
        copy_rims(refs[8], out_a, out_b, 2 * HALF)

def visit(halves, sides, rims, first, second, following, flat, rim_at, second_at):
    vmem = pl.BlockSpec(memory_space=pltpu.VMEM)
    kind = halves[0].dtype
    lines = 2 * HALF
    if following is not None:
        lines += HB * (4 * TILE + 8)
    shape = jax.ShapeDtypeStruct((HALF, 2 * TILE) if flat else (lines, TILE), kind)
    operands = [*halves, *sides, *rims, first, second]
    if following is not None:
        operands.append(following)
    return pl.pallas_call(
        functools.partial(visit_kernel, rim_at, second_at, flat),
        out_shape=(shape, shape),
        in_specs=[vmem] * len(operands),
        out_specs=(vmem, vmem),
        scratch_shapes=[
            pltpu.VMEM((17 * TILE, 2 * TILE), kind),
            pltpu.VMEM((13 * TILE, 2 * TILE), kind),
        ],
        compiler_params=pltpu.CompilerParams(vmem_limit_bytes=24 * 1024 * 1024),
        cost_estimate=pl.CostEstimate(flops=700_000_000, bytes_accessed=4_000_000, transcendentals=0),
        name="two_steps",
    )(*operands)

def pack_kernel(total, info, cols, counts, blocks, packed, rim_a, rim_b):
    even = info[0]
    block_rows, slots = cols.shape
    span = slots * TILE
    lines = block_rows * span
    line = lax.broadcasted_iota(jnp.int32, (8, TILE), 0)
    for c in range(0, block_rows, 2):
        tables = []
        for i in range(2):
            source = jnp.where(even == 1, block_rows - 1 - (c + i), c + i)
            packed[(c + i) * span : (c + i + 1) * span, :] = blocks[
                pl.ds(pl.multiple_of(source * span, span), span), :
            ]
            table = jnp.full((8, TILE), DEAD, jnp.int32)
            for j in range(slots):
                offset = lax.rem(cols[source, j] - info[1] - source + HB + total, total)
                offset = jnp.where(even == 1, 2 * HB - offset, offset)
                value = jnp.where(j < counts[source], offset, DEAD)
                table = jnp.where(line == j, value, table)
            tables.append(table.astype(jnp.float32))
        both = jnp.concatenate(tables, axis=0).astype(packed.dtype)
        packed[lines + c * 8 : lines + c * 8 + 16, :] = both
    edge = HB * span
    rim_a[:edge, :] = packed[:edge, :]
    rim_a[edge:, :] = packed[lines : lines + 8 * HB, :]
    rim_b[:edge, :] = packed[lines - edge : lines, :]
    rim_b[edge:, :] = packed[lines + 8 * (block_rows - HB) :, :]

def pack(total, info, cols, counts, blocks):
    block_rows, slots, tile, _ = blocks.shape
    lines = block_rows * slots * tile
    vmem = pl.BlockSpec(memory_space=pltpu.VMEM)
    smem = pl.BlockSpec(memory_space=pltpu.SMEM)
    rim = jax.ShapeDtypeStruct((HB * slots * tile + 8 * HB, tile), blocks.dtype)
    whole = jax.ShapeDtypeStruct((lines + 8 * block_rows, tile), blocks.dtype)
    return pl.pallas_call(
        functools.partial(pack_kernel, total),
        out_shape=(whole, rim, rim),
        in_specs=[smem, smem, smem, vmem],
        out_specs=(vmem, vmem, vmem),
        compiler_params=pltpu.CompilerParams(vmem_limit_bytes=16 * 1024 * 1024),
        name="pack_operator",
    )(info, cols, counts, blocks.reshape(lines, tile))

def halve_kernel(info, start, half_a, half_b):
    block_rows = start.shape[0] // TILE
    for c in range(block_rows):
        source = jnp.where(info[0] == 1, block_rows - 1 - c, c)
        half = half_a if c < 4 else half_b
        value = start[pl.ds(pl.multiple_of(source * TILE, TILE), TILE), :]
        at = c % 4 * TILE
        half[at : at + TILE, :] = value[:, :TILE]
        half[HALF + at : HALF + at + TILE, :] = value[:, TILE:]

def halve(info, start):
    vmem = pl.BlockSpec(memory_space=pltpu.VMEM)
    half = jax.ShapeDtypeStruct((2 * HALF, TILE), start.dtype)
    return pl.pallas_call(
        halve_kernel,
        out_shape=(half, half),
        in_specs=[pl.BlockSpec(memory_space=pltpu.SMEM), vmem],
        out_specs=(vmem, vmem),
        compiler_params=pltpu.CompilerParams(vmem_limit_bytes=8 * 1024 * 1024),
        name="halve_start",
    )(info, start)

def swap_kernel(info, *refs):
    operators, swapped = refs[:-1], refs[-1]
    span = operators[0].shape[0]
    for n, (operator, following) in enumerate(zip(operators[:-1], operators[1:])):
        @pl.loop(0, span, step=160)
        def _(line):
            at = pl.ds(pl.multiple_of(line, 32), 160)
            to = pl.ds(pl.multiple_of(n * span + line, 32), 160)
            swapped[to, :] = jnp.where(info[2] == 0, following[at, :], operator[at, :])

def gather_swap(info, operators):
    vmem = pl.BlockSpec(memory_space=pltpu.VMEM)
    lines = (len(operators) - 1) * operators[0].shape[0]
    return pl.pallas_call(
        swap_kernel,
        out_shape=jax.ShapeDtypeStruct((lines, TILE), operators[0].dtype),
        in_specs=[pl.BlockSpec(memory_space=pltpu.SMEM)] + [vmem] * len(operators),
        out_specs=vmem,
        compiler_params=pltpu.CompilerParams(vmem_limit_bytes=24 * 1024 * 1024),
        name="gather_swap",
    )(info, *operators)

def rims_kernel(*refs):
    operators, (side_a, side_b) = refs[:-2], refs[-2:]
    for n, operator in enumerate(operators):
        copy_rims(operator, side_a, side_b, n * HB * (4 * TILE + 8))

def gather_rims(operators):
    vmem = pl.BlockSpec(memory_space=pltpu.VMEM)
    lines = len(operators) * HB * (4 * TILE + 8)
    side = jax.ShapeDtypeStruct((lines, TILE), operators[0].dtype)
    return pl.pallas_call(
        rims_kernel,
        out_shape=(side, side),
        in_specs=[vmem] * len(operators),
        out_specs=(vmem, vmem),
        compiler_params=pltpu.CompilerParams(vmem_limit_bytes=24 * 1024 * 1024),
        name="gather_rims",
    )(*operators)


NB = 16

def factor_kernel(info, gram_ref, half_a, half_b, basis_ref, factor_ref, a_ref, w_ref):
    size = gram_ref.shape[0]
    a_ref[...] = gram_ref[...]
    row_i = lax.broadcasted_iota(jnp.int32, (size, size), 0)
    col_i = lax.broadcasted_iota(jnp.int32, (size, size), 1)
    w_ref[...] = jnp.where(row_i == col_i, 1.0, 0.0)
    lanes = 128
    sub = lax.broadcasted_iota(jnp.int32, (NB, lanes), 0)
    wide_row = lax.broadcasted_iota(jnp.int32, (NB, size), 0)
    wide_col = lax.broadcasted_iota(jnp.int32, (NB, size), 1)
    for first in range(0, size, NB):
        panel = a_ref[first : first + NB, :]
        other = w_ref[first : first + NB, :]
        columns = [
            jnp.broadcast_to(panel[:, first + k : first + k + 1], (NB, lanes))
            for k in range(NB)
        ]
        pivots = jnp.zeros((NB, lanes), jnp.float32)
        for j in range(NB):
            column = columns[j]
            pivot = jnp.broadcast_to(column[j : j + 1, :], (NB, lanes))
            pivots = jnp.where(sub == j, pivot, pivots)
            if j == NB - 1:
                break
            scaled = jnp.where(sub > j, column / pivot, 0.0)
            for k in range(j + 1, NB):
                columns[k] = columns[k] - scaled * jnp.broadcast_to(
                    column[k : k + 1, :], (NB, lanes)
                )
            both = jnp.concatenate([scaled] * (size // lanes), axis=1)
            panel = panel - both * jnp.broadcast_to(panel[j : j + 1, :], (NB, size))
            other = other - both * jnp.broadcast_to(other[j : j + 1, :], (NB, size))
        scale = 1.0 / jnp.sqrt(pivots)
        both = jnp.concatenate([scale] * (size // lanes), axis=1)
        upper = jnp.where(wide_col >= wide_row + first, panel * both, 0.0)
        other = other * both
        factor_ref[first : first + NB, :] = upper
        w_ref[first : first + NB, :] = other
        rest = first + NB
        if rest < size:
            low_row = rest // lanes * lanes
            low_lane = first // lanes * lanes
            high_lane = low_lane + lanes
            right = jnp.concatenate([upper[:, low_lane:], other[:, :high_lane]], axis=1)
            change = lax.dot_general(
                upper[:, low_row:], right, (((0,), (0,)), ((), ())),
                preferred_element_type=jnp.float32, precision=lax.Precision.HIGHEST,
            )[rest - low_row :, :]
            split = size - low_lane
            a_ref[rest:, low_lane:] = a_ref[rest:, low_lane:] - change[:, :split]
            w_ref[rest:, :high_lane] = w_ref[rest:, :high_lane] - change[:, split:]
    w = w_ref[...]
    high = w.astype(jnp.bfloat16)
    low = (w - high.astype(jnp.float32)).astype(jnp.bfloat16)
    dims = (((1,), (1,)), ((), ()))
    for c in range(8):
        half = half_a if c < 4 else half_b
        rows = half[c % 4 * TILE : (c % 4 + 1) * TILE, :]
        place = jnp.where(info[0] == 1, 7 - c, c)
        basis_ref[pl.ds(pl.multiple_of(place * TILE, TILE), TILE), :] = lax.dot_general(
            rows, high, dims, preferred_element_type=jnp.float32
        ) + lax.dot_general(rows, low, dims, preferred_element_type=jnp.float32)

def finish(info, gram, halves):
    size = gram.shape[0]
    vmem = pl.BlockSpec(memory_space=pltpu.VMEM)
    return pl.pallas_call(
        factor_kernel,
        out_shape=(
            jax.ShapeDtypeStruct((2 * HALF, size), jnp.float32),
            jax.ShapeDtypeStruct((size, size), jnp.float32),
        ),
        in_specs=[pl.BlockSpec(memory_space=pltpu.SMEM), vmem, vmem, vmem],
        out_specs=(vmem, vmem),
        scratch_shapes=[pltpu.VMEM((size, size), jnp.float32), pltpu.VMEM((size, size), jnp.float32)],
        name="factor_solve",
    )(info, gram, *halves)


def sum_over_rows(term):
    owners = lax.axis_size("rows")
    size = term.shape[0]
    pieces = term.reshape(owners, size // owners, size)
    pieces = lax.all_to_all(pieces, "rows", 0, 0, tiled=True)
    mine = jnp.sum(pieces.astype(jnp.float32), axis=0, keepdims=True)
    copies = jnp.broadcast_to(mine, (owners, size // owners, size))
    return lax.all_to_all(copies, "rows", 0, 0, tiled=True).reshape(size, size)


def body(start, blocks, cols, counts):
    block_rows, _, _ = blocks.shape[1:4]
    rows_here = start.shape[1]
    owners = lax.axis_size("rows")
    sections = lax.axis_size("phase")
    place = lax.axis_index("rows")
    core = lax.axis_index("phase") % 2
    info = jnp.stack([1 - place % 2, place * block_rows, core]).astype(jnp.int32)
    first_core = core == 0
    to_a = [(i, i ^ 1) for i in range(owners)]
    to_b = [(i, (i + 1) % owners if i % 2 else (i - 1) % owners) for i in range(owners)]
    back = [(i, (i - 2) % sections) for i in range(sections)]
    ahead = [(i, (i + 2) % sections) for i in range(sections)]
    mates = [(i, i ^ 1) for i in range(sections)]

    def rims(a_side, b_side):
        return (lax.ppermute(a_side, "rows", to_a), lax.ppermute(b_side, "rows", to_b))

    visits = sections // 2
    far = visits // 2
    home, home_a, home_b = pack(block_rows * owners, info, cols[0], counts[0], blocks[0])
    held = {0: home, visits: home}
    held[1] = lax.ppermute(home, "phase", back)
    held[visits - 1] = lax.ppermute(home, "phase", ahead)
    halves = halve(info, start[0])
    first_rims = rims(home_a, home_b)
    span = home.shape[0]
    rim_span = home_a.shape[0]
    batched = far + 2
    for turn in range(visits):
        sides = (
            lax.ppermute(halves[0], "rows", to_a), lax.ppermute(halves[1], "rows", to_b)
        )
        second_at = 0
        if turn <= far:
            here, later, halves = lax.optimization_barrier((held[turn], held[turn + 1], halves))
            if turn + 2 <= far:
                held[turn + 2] = lax.ppermute(later, "phase", back)
            end = visits - 1 - turn
            if turn > 0 and end > far:
                nearer, halves = lax.optimization_barrier((held[end + 1], halves))
                held[end] = lax.ppermute(nearer, "phase", ahead)
            picked = jnp.where(first_core, later, here)
            other = lax.ppermute(picked, "phase", mates)
        if turn == far - 1:
            last, halves = lax.optimization_barrier(
                ([held[n] for n in range(batched, visits)], halves)
            )
            last_rims = rims(*gather_rims(last))
        if turn == far:
            last = [later] + [held[n] for n in range(batched, visits)] + [home]
            others = lax.ppermute(gather_swap(info, last), "phase", mates)
        if turn > far:
            other, second_at = others, (turn - far - 1) * span
        if turn == 0:
            rim, rim_at = first_rims, 0
        elif turn < batched:
            rim, rim_at = sides, rows_here
        else:
            rim, rim_at = last_rims, (turn - batched) * rim_span
        halves = visit(
            halves, sides, rim, held[turn], other,
            held[turn + 1] if turn + 1 < batched else None,
            turn + 1 == visits, rim_at, second_at,
        )

    arrived = jnp.concatenate(halves, axis=0)
    gram_term = lax.dot_general(
        arrived, arrived, (((0,), (0,)), ((), ())), preferred_element_type=jnp.float32
    )
    gram_total = sum_over_rows(gram_term.astype(jnp.bfloat16)) / (rows_here * owners)
    basis_out, upper_factor = finish(info, gram_total, halves)
    return (basis_out[None], upper_factor[None])


def solution(mesh):
    placed = (
        P("phase", "rows", None),
        P("phase", "rows", None, None, None),
        P("phase", "rows", None),
        P("phase", "rows"),
    )
    return jax.shard_map(
        body,
        mesh=mesh,
        in_specs=placed,
        out_specs=(P("phase", "rows", None), P("phase", None, None)),
        check_vma=False,
    )
```

```python
import functools

import jax
import jax.numpy as jnp
from jax import lax
from jax.experimental import pallas as pl
from jax.experimental.pallas import tpu as pltpu
from jax.sharding import PartitionSpec as P


HB = 2
TILE = 128
HALF = 4 * TILE
DEAD = 7

def copy_rims(operator, side_a, side_b, at):
    span = operator.shape[0]
    body = span - span // (4 * TILE + 8) * 8
    edge = HB * 4 * TILE
    tables = 8 * HB

    @pl.loop(0, edge, step=TILE)
    def _(line):
        line = pl.multiple_of(line, TILE)
        to = pl.ds(pl.multiple_of(at + line, 16), TILE)
        side_a[to, :] = operator[pl.ds(line, TILE), :]
        side_b[to, :] = operator[pl.ds(body - edge + line, TILE), :]

    at = at + edge
    side_a[at : at + tables, :] = operator[body : body + tables, :]
    side_b[at : at + tables, :] = operator[span - tables :, :]

def visit_kernel(rim_at, second_at, flat, *refs):
    cur_a, cur_b, ra, rb, rim_a, rim_b, first, second = refs[:8]
    out_a, out_b, wide, mid = refs[-4:]

    def pieces(ref, n):
        for part in range(2):
            at = part * HALF + n * TILE
            yield slice(part * TILE, (part + 1) * TILE), ref[at : at + TILE, :]

    for n in range(4):
        for place, ref in ((3 - n, ra), (15 - n, rb), (4 + n, cur_a), (8 + n, cur_b)):
            for lanes, piece in pieces(ref, n):
                wide[place * TILE : (place + 1) * TILE, lanes] = piece
    zero = jnp.zeros((TILE, 2 * TILE), wide.dtype)
    wide[16 * TILE :, :] = zero
    mid[12 * TILE :, :] = zero

    def row(ops, at, count, n, source, centre, sign, nothing):
        line = at + count * 4 * TILE + n * 8
        table = ops[line : line + 8, :].astype(jnp.float32).astype(jnp.int32)

        def block(j):
            if j == 0:
                return source[centre * TILE : (centre + 1) * TILE, :]
            value = jnp.max(table[j : j + 1, :])
            place = jnp.where(value == DEAD, nothing, centre + sign * (value - 2))
            return source[pl.ds(pl.multiple_of(place * TILE, TILE), TILE), :]

        def slot(j):
            return ops[at + (n * 4 + j) * TILE : at + (n * 4 + j + 1) * TILE, :]

        total = None
        for j in (0, 2):
            left = jnp.concatenate([slot(j), slot(j + 1)], axis=1)
            right = jnp.concatenate([block(j), block(j + 1)], axis=0)
            part = jnp.dot(left, right, preferred_element_type=jnp.float32)
            total = part if total is None else total + part
        return total.astype(out_a.dtype)

    for n in range(2):
        c = 1 - n
        mid[c * TILE : (c + 1) * TILE, :] = row(rim_a, rim_at, 2, n, wide, c + 2, -1, 16)
        c = 11 - n
        mid[c * TILE : (c + 1) * TILE, :] = row(rim_b, rim_at, 2, n, wide, c + 2, -1, 16)
    for c in range(8):
        mid[(c + 2) * TILE : (c + 3) * TILE, :] = row(first, 0, 8, c, wide, c + 4, 1, 16)
    for c in range(8):
        half = out_a if c < 4 else out_b
        value = row(second, second_at, 8, c, mid, c + 2, 1, 12)
        at = c % 4 * TILE
        if flat:
            half[at : at + TILE, :] = value
        else:
            half[at : at + TILE, :] = value[:, :TILE]
            half[HALF + at : HALF + at + TILE, :] = value[:, TILE:]
    for n, operator in enumerate(refs[8:-4]):
        copy_rims(operator, out_a, out_b, 2 * HALF + n * HB * (4 * TILE + 8))

def visit(halves, sides, rims, first, second, following, flat, rim_at, second_at):
    vmem = pl.BlockSpec(memory_space=pltpu.VMEM)
    kind = halves[0].dtype
    lines = 2 * HALF
    lines += len(following) * HB * (4 * TILE + 8)
    shape = jax.ShapeDtypeStruct((HALF, 2 * TILE) if flat else (lines, TILE), kind)
    operands = [*halves, *sides, *rims, first, second, *following]
    return pl.pallas_call(
        functools.partial(visit_kernel, rim_at, second_at, flat),
        out_shape=(shape, shape),
        in_specs=[vmem] * len(operands),
        out_specs=(vmem, vmem),
        scratch_shapes=[
            pltpu.VMEM((17 * TILE, 2 * TILE), kind),
            pltpu.VMEM((13 * TILE, 2 * TILE), kind),
        ],
        compiler_params=pltpu.CompilerParams(vmem_limit_bytes=24 * 1024 * 1024),
        cost_estimate=pl.CostEstimate(flops=700_000_000, bytes_accessed=4_000_000, transcendentals=0),
        name="two_steps",
    )(*operands)

def pack_kernel(total, info, cols, counts, blocks, packed, rim_a, rim_b):
    even = info[0]
    block_rows, slots = cols.shape
    span = slots * TILE
    lines = block_rows * span
    line = lax.broadcasted_iota(jnp.int32, (8, TILE), 0)
    for c in range(0, block_rows, 2):
        tables = []
        for i in range(2):
            source = jnp.where(even == 1, block_rows - 1 - (c + i), c + i)
            packed[(c + i) * span : (c + i + 1) * span, :] = blocks[
                pl.ds(pl.multiple_of(source * span, span), span), :
            ]
            table = jnp.full((8, TILE), DEAD, jnp.int32)
            for j in range(slots):
                offset = lax.rem(cols[source, j] - info[1] - source + HB + total, total)
                offset = jnp.where(even == 1, 2 * HB - offset, offset)
                value = jnp.where(j < counts[source], offset, DEAD)
                table = jnp.where(line == j, value, table)
            tables.append(table.astype(jnp.float32))
        both = jnp.concatenate(tables, axis=0).astype(packed.dtype)
        packed[lines + c * 8 : lines + c * 8 + 16, :] = both
    edge = HB * span
    rim_a[:edge, :] = packed[:edge, :]
    rim_a[edge:, :] = packed[lines : lines + 8 * HB, :]
    rim_b[:edge, :] = packed[lines - edge : lines, :]
    rim_b[edge:, :] = packed[lines + 8 * (block_rows - HB) :, :]

def pack(total, info, cols, counts, blocks):
    block_rows, slots, tile, _ = blocks.shape
    lines = block_rows * slots * tile
    vmem = pl.BlockSpec(memory_space=pltpu.VMEM)
    smem = pl.BlockSpec(memory_space=pltpu.SMEM)
    rim = jax.ShapeDtypeStruct((HB * slots * tile + 8 * HB, tile), blocks.dtype)
    whole = jax.ShapeDtypeStruct((lines + 8 * block_rows, tile), blocks.dtype)
    return pl.pallas_call(
        functools.partial(pack_kernel, total),
        out_shape=(whole, rim, rim),
        in_specs=[smem, smem, smem, vmem],
        out_specs=(vmem, vmem, vmem),
        compiler_params=pltpu.CompilerParams(vmem_limit_bytes=16 * 1024 * 1024),
        name="pack_operator",
    )(info, cols, counts, blocks.reshape(lines, tile))

def halve_kernel(info, start, half_a, half_b):
    block_rows = start.shape[0] // TILE
    for c in range(block_rows):
        source = jnp.where(info[0] == 1, block_rows - 1 - c, c)
        half = half_a if c < 4 else half_b
        value = start[pl.ds(pl.multiple_of(source * TILE, TILE), TILE), :]
        at = c % 4 * TILE
        half[at : at + TILE, :] = value[:, :TILE]
        half[HALF + at : HALF + at + TILE, :] = value[:, TILE:]

def halve(info, start):
    vmem = pl.BlockSpec(memory_space=pltpu.VMEM)
    half = jax.ShapeDtypeStruct((2 * HALF, TILE), start.dtype)
    return pl.pallas_call(
        halve_kernel,
        out_shape=(half, half),
        in_specs=[pl.BlockSpec(memory_space=pltpu.SMEM), vmem],
        out_specs=(vmem, vmem),
        compiler_params=pltpu.CompilerParams(vmem_limit_bytes=8 * 1024 * 1024),
        name="halve_start",
    )(info, start)

def swap_kernel(info, *refs):
    operators, swapped = refs[:-1], refs[-1]
    span = operators[0].shape[0]
    for n, (operator, following) in enumerate(zip(operators[:-1], operators[1:])):
        @pl.loop(0, span, step=160)
        def _(line):
            at = pl.ds(pl.multiple_of(line, 32), 160)
            to = pl.ds(pl.multiple_of(n * span + line, 32), 160)
            swapped[to, :] = jnp.where(info[2] == 0, following[at, :], operator[at, :])

def gather_swap(info, operators):
    vmem = pl.BlockSpec(memory_space=pltpu.VMEM)
    lines = (len(operators) - 1) * operators[0].shape[0]
    return pl.pallas_call(
        swap_kernel,
        out_shape=jax.ShapeDtypeStruct((lines, TILE), operators[0].dtype),
        in_specs=[pl.BlockSpec(memory_space=pltpu.SMEM)] + [vmem] * len(operators),
        out_specs=vmem,
        compiler_params=pltpu.CompilerParams(vmem_limit_bytes=24 * 1024 * 1024),
        name="gather_swap",
    )(info, *operators)


NB = 16

def factor_kernel(info, gram_ref, half_a, half_b, basis_ref, factor_ref, a_ref, w_ref):
    size = gram_ref.shape[0]
    a_ref[...] = gram_ref[...]
    row_i = lax.broadcasted_iota(jnp.int32, (size, size), 0)
    col_i = lax.broadcasted_iota(jnp.int32, (size, size), 1)
    w_ref[...] = jnp.where(row_i == col_i, 1.0, 0.0)
    lanes = 128
    sub = lax.broadcasted_iota(jnp.int32, (NB, lanes), 0)
    wide_row = lax.broadcasted_iota(jnp.int32, (NB, size), 0)
    wide_col = lax.broadcasted_iota(jnp.int32, (NB, size), 1)
    for first in range(0, size, NB):
        panel = a_ref[first : first + NB, :]
        other = w_ref[first : first + NB, :]
        columns = [
            jnp.broadcast_to(panel[:, first + k : first + k + 1], (NB, lanes))
            for k in range(NB)
        ]
        pivots = jnp.zeros((NB, lanes), jnp.float32)
        for j in range(NB):
            column = columns[j]
            pivot = jnp.broadcast_to(column[j : j + 1, :], (NB, lanes))
            pivots = jnp.where(sub == j, pivot, pivots)
            if j == NB - 1:
                break
            scaled = jnp.where(sub > j, column / pivot, 0.0)
            for k in range(j + 1, NB):
                columns[k] = columns[k] - scaled * jnp.broadcast_to(
                    column[k : k + 1, :], (NB, lanes)
                )
            both = jnp.concatenate([scaled] * (size // lanes), axis=1)
            panel = panel - both * jnp.broadcast_to(panel[j : j + 1, :], (NB, size))
            other = other - both * jnp.broadcast_to(other[j : j + 1, :], (NB, size))
        scale = 1.0 / jnp.sqrt(pivots)
        both = jnp.concatenate([scale] * (size // lanes), axis=1)
        upper = jnp.where(wide_col >= wide_row + first, panel * both, 0.0)
        other = other * both
        factor_ref[first : first + NB, :] = upper
        w_ref[first : first + NB, :] = other
        rest = first + NB
        if rest < size:
            low_row = rest // lanes * lanes
            low_lane = first // lanes * lanes
            high_lane = low_lane + lanes
            right = jnp.concatenate([upper[:, low_lane:], other[:, :high_lane]], axis=1)
            change = lax.dot_general(
                upper[:, low_row:], right, (((0,), (0,)), ((), ())),
                preferred_element_type=jnp.float32, precision=lax.Precision.HIGHEST,
            )[rest - low_row :, :]
            split = size - low_lane
            a_ref[rest:, low_lane:] = a_ref[rest:, low_lane:] - change[:, :split]
            w_ref[rest:, :high_lane] = w_ref[rest:, :high_lane] - change[:, split:]
    w = w_ref[...]
    high = w.astype(jnp.bfloat16)
    low = (w - high.astype(jnp.float32)).astype(jnp.bfloat16)
    dims = (((1,), (1,)), ((), ()))
    for c in range(8):
        half = half_a if c < 4 else half_b
        rows = half[c % 4 * TILE : (c % 4 + 1) * TILE, :]
        place = jnp.where(info[0] == 1, 7 - c, c)
        basis_ref[pl.ds(pl.multiple_of(place * TILE, TILE), TILE), :] = lax.dot_general(
            rows, high, dims, preferred_element_type=jnp.float32
        ) + lax.dot_general(rows, low, dims, preferred_element_type=jnp.float32)

def finish(info, gram, halves):
    size = gram.shape[0]
    vmem = pl.BlockSpec(memory_space=pltpu.VMEM)
    return pl.pallas_call(
        factor_kernel,
        out_shape=(
            jax.ShapeDtypeStruct((2 * HALF, size), jnp.float32),
            jax.ShapeDtypeStruct((size, size), jnp.float32),
        ),
        in_specs=[pl.BlockSpec(memory_space=pltpu.SMEM), vmem, vmem, vmem],
        out_specs=(vmem, vmem),
        scratch_shapes=[pltpu.VMEM((size, size), jnp.float32), pltpu.VMEM((size, size), jnp.float32)],
        name="factor_solve",
    )(info, gram, *halves)


def sum_over_rows(term):
    owners = lax.axis_size("rows")
    size = term.shape[0]
    pieces = term.reshape(owners, size // owners, size)
    pieces = lax.all_to_all(pieces, "rows", 0, 0, tiled=True)
    mine = jnp.sum(pieces.astype(jnp.float32), axis=0, keepdims=True)
    copies = jnp.broadcast_to(mine, (owners, size // owners, size))
    return lax.all_to_all(copies, "rows", 0, 0, tiled=True).reshape(size, size)


def body(start, blocks, cols, counts):
    block_rows, _, _ = blocks.shape[1:4]
    rows_here = start.shape[1]
    owners = lax.axis_size("rows")
    sections = lax.axis_size("phase")
    place = lax.axis_index("rows")
    core = lax.axis_index("phase") % 2
    info = jnp.stack([1 - place % 2, place * block_rows, core]).astype(jnp.int32)
    first_core = core == 0
    to_a = [(i, i ^ 1) for i in range(owners)]
    to_b = [(i, (i + 1) % owners if i % 2 else (i - 1) % owners) for i in range(owners)]
    back = [(i, (i - 2) % sections) for i in range(sections)]
    ahead = [(i, (i + 2) % sections) for i in range(sections)]
    mates = [(i, i ^ 1) for i in range(sections)]

    def rims(a_side, b_side):
        return (lax.ppermute(a_side, "rows", to_a), lax.ppermute(b_side, "rows", to_b))

    visits = sections // 2
    far = visits // 2
    home, home_a, home_b = pack(block_rows * owners, info, cols[0], counts[0], blocks[0])
    held = {0: home, visits: home}
    held[1] = lax.ppermute(home, "phase", back)
    held[visits - 1] = lax.ppermute(home, "phase", ahead)
    halves = halve(info, start[0])
    first_rims = rims(home_a, home_b)
    span = home.shape[0]
    rim_span = home_a.shape[0]
    riders = {n: [n] for n in range(1, far + 2)}
    for n in range(far + 2, visits):
        riders[visits + 1 - n].append(n)
    rim_of = {0: (first_rims, 0)}
    for turn in range(visits):
        sides = (lax.ppermute(halves[0], "rows", to_a), lax.ppermute(halves[1], "rows", to_b))
        second_at = 0
        if turn <= far:
            here, later, halves = lax.optimization_barrier((held[turn], held[turn + 1], halves))
            if turn + 2 <= far:
                held[turn + 2] = lax.ppermute(later, "phase", back)
            end = visits - 1 - turn
            if turn > 0 and end > far:
                nearer, halves = lax.optimization_barrier((held[end + 1], halves))
                held[end] = lax.ppermute(nearer, "phase", ahead)
            picked = jnp.where(first_core, later, here)
            other = lax.ppermute(picked, "phase", mates)
        if turn == far:
            last = [later] + [held[n] for n in range(turn + 2, visits)] + [home]
            others = lax.ppermute(gather_swap(info, last), "phase", mates)
        if turn > far:
            other, second_at = others, (turn - far - 1) * span
        for n, operator in enumerate(riders.get(turn, [])):
            rim_of[operator] = (sides, rows_here + n * rim_span)
        rim, rim_at = rim_of[turn]
        following = [held[n] for n in riders.get(turn + 1, [])]
        halves = visit(
            halves, sides, rim, held[turn], other, following,
            turn + 1 == visits, rim_at, second_at,
        )

    arrived = jnp.concatenate(halves, axis=0)
    gram_term = lax.dot_general(
        arrived, arrived, (((0,), (0,)), ((), ())), preferred_element_type=jnp.float32
    )
    gram_total = sum_over_rows(gram_term.astype(jnp.bfloat16)) / (rows_here * owners)
    basis_out, upper_factor = finish(info, gram_total, halves)
    return (basis_out[None], upper_factor[None])


def solution(mesh):
    placed = (
        P("phase", "rows", None),
        P("phase", "rows", None, None, None),
        P("phase", "rows", None),
        P("phase", "rows"),
    )
    return jax.shard_map(
        body,
        mesh=mesh,
        in_specs=placed,
        out_specs=(P("phase", "rows", None), P("phase", None, None)),
        check_vma=False,
    )
```

```python
import functools

import jax
import jax.numpy as jnp
from jax import lax
from jax.experimental import pallas as pl
from jax.experimental.pallas import tpu as pltpu
from jax.sharding import PartitionSpec as P


HB = 2
TILE = 128
HALF = 4 * TILE
DEAD = 7

def copy_rims(operator, side_a, side_b, at):
    span = operator.shape[0]
    body = span - span // (4 * TILE + 8) * 8
    edge = HB * 4 * TILE
    tables = 8 * HB

    @pl.loop(0, edge, step=TILE)
    def _(line):
        line = pl.multiple_of(line, TILE)
        to = pl.ds(pl.multiple_of(at + line, 16), TILE)
        side_a[to, :] = operator[pl.ds(line, TILE), :]
        side_b[to, :] = operator[pl.ds(body - edge + line, TILE), :]

    at = at + edge
    side_a[at : at + tables, :] = operator[body : body + tables, :]
    side_b[at : at + tables, :] = operator[span - tables :, :]

def visit_kernel(rim_at, second_at, flat, *refs):
    cur_a, cur_b, ra, rb, rim_a, rim_b, first, second = refs[:8]
    out_a, out_b, wide, mid = refs[-4:]

    def pieces(ref, n):
        for part in range(2):
            at = part * HALF + n * TILE
            yield slice(part * TILE, (part + 1) * TILE), ref[at : at + TILE, :]

    for n in range(4):
        for place, ref in ((3 - n, ra), (15 - n, rb), (4 + n, cur_a), (8 + n, cur_b)):
            for lanes, piece in pieces(ref, n):
                wide[place * TILE : (place + 1) * TILE, lanes] = piece
    zero = jnp.zeros((TILE, 2 * TILE), wide.dtype)
    wide[16 * TILE :, :] = zero
    mid[12 * TILE :, :] = zero

    def row(ops, at, count, n, source, centre, sign, nothing):
        line = at + count * 4 * TILE + n * 8
        table = ops[line : line + 8, :].astype(jnp.float32).astype(jnp.int32)

        def block(j):
            if j == 0:
                return source[centre * TILE : (centre + 1) * TILE, :]
            value = jnp.max(table[j : j + 1, :])
            place = jnp.where(value == DEAD, nothing, centre + sign * (value - 2))
            return source[pl.ds(pl.multiple_of(place * TILE, TILE), TILE), :]

        def slot(j):
            return ops[at + (n * 4 + j) * TILE : at + (n * 4 + j + 1) * TILE, :]

        total = None
        for j in (0, 2):
            left = jnp.concatenate([slot(j), slot(j + 1)], axis=1)
            right = jnp.concatenate([block(j), block(j + 1)], axis=0)
            part = jnp.dot(left, right, preferred_element_type=jnp.float32)
            total = part if total is None else total + part
        return total.astype(out_a.dtype)

    for n in range(2):
        c = 1 - n
        mid[c * TILE : (c + 1) * TILE, :] = row(rim_a, rim_at, 2, n, wide, c + 2, -1, 16)
        c = 11 - n
        mid[c * TILE : (c + 1) * TILE, :] = row(rim_b, rim_at, 2, n, wide, c + 2, -1, 16)
    for c in range(8):
        mid[(c + 2) * TILE : (c + 3) * TILE, :] = row(first, 0, 8, c, wide, c + 4, 1, 16)
    for c in range(8):
        half = out_a if c < 4 else out_b
        value = row(second, second_at, 8, c, mid, c + 2, 1, 12)
        at = c % 4 * TILE
        if flat:
            half[at : at + TILE, :] = value
        else:
            half[at : at + TILE, :] = value[:, :TILE]
            half[HALF + at : HALF + at + TILE, :] = value[:, TILE:]
    for n, operator in enumerate(refs[8:-4]):
        copy_rims(operator, out_a, out_b, 2 * HALF + n * HB * (4 * TILE + 8))

def visit(halves, sides, rims, first, second, following, flat, rim_at, second_at):
    vmem = pl.BlockSpec(memory_space=pltpu.VMEM)
    kind = halves[0].dtype
    lines = 2 * HALF
    lines += len(following) * HB * (4 * TILE + 8)
    shape = jax.ShapeDtypeStruct((HALF, 2 * TILE) if flat else (lines, TILE), kind)
    operands = [*halves, *sides, *rims, first, second, *following]
    return pl.pallas_call(
        functools.partial(visit_kernel, rim_at, second_at, flat),
        out_shape=(shape, shape),
        in_specs=[vmem] * len(operands),
        out_specs=(vmem, vmem),
        scratch_shapes=[
            pltpu.VMEM((17 * TILE, 2 * TILE), kind),
            pltpu.VMEM((13 * TILE, 2 * TILE), kind),
        ],
        compiler_params=pltpu.CompilerParams(vmem_limit_bytes=24 * 1024 * 1024),
        cost_estimate=pl.CostEstimate(flops=700_000_000, bytes_accessed=4_000_000, transcendentals=0),
        name="two_steps",
    )(*operands)

def pack_kernel(total, info, cols, counts, blocks, packed, rim_a, rim_b):
    even = info[0]
    block_rows, slots = cols.shape
    span = slots * TILE
    lines = block_rows * span
    line = lax.broadcasted_iota(jnp.int32, (8, TILE), 0)
    for c in range(0, block_rows, 2):
        tables = []
        for i in range(2):
            source = jnp.where(even == 1, block_rows - 1 - (c + i), c + i)
            packed[(c + i) * span : (c + i + 1) * span, :] = blocks[
                pl.ds(pl.multiple_of(source * span, span), span), :
            ]
            table = jnp.full((8, TILE), DEAD, jnp.int32)
            for j in range(slots):
                offset = lax.rem(cols[source, j] - info[1] - source + HB + total, total)
                offset = jnp.where(even == 1, 2 * HB - offset, offset)
                value = jnp.where(j < counts[source], offset, DEAD)
                table = jnp.where(line == j, value, table)
            tables.append(table.astype(jnp.float32))
        both = jnp.concatenate(tables, axis=0).astype(packed.dtype)
        packed[lines + c * 8 : lines + c * 8 + 16, :] = both
    edge = HB * span
    rim_a[:edge, :] = packed[:edge, :]
    rim_a[edge:, :] = packed[lines : lines + 8 * HB, :]
    rim_b[:edge, :] = packed[lines - edge : lines, :]
    rim_b[edge:, :] = packed[lines + 8 * (block_rows - HB) :, :]

def pack(total, info, cols, counts, blocks):
    block_rows, slots, tile, _ = blocks.shape
    lines = block_rows * slots * tile
    vmem = pl.BlockSpec(memory_space=pltpu.VMEM)
    smem = pl.BlockSpec(memory_space=pltpu.SMEM)
    rim = jax.ShapeDtypeStruct((HB * slots * tile + 8 * HB, tile), blocks.dtype)
    whole = jax.ShapeDtypeStruct((lines + 8 * block_rows, tile), blocks.dtype)
    return pl.pallas_call(
        functools.partial(pack_kernel, total),
        out_shape=(whole, rim, rim),
        in_specs=[smem, smem, smem, vmem],
        out_specs=(vmem, vmem, vmem),
        compiler_params=pltpu.CompilerParams(vmem_limit_bytes=16 * 1024 * 1024),
        name="pack_operator",
    )(info, cols, counts, blocks.reshape(lines, tile))

def halve_kernel(info, start, half_a, half_b):
    block_rows = start.shape[0] // TILE
    for c in range(block_rows):
        source = jnp.where(info[0] == 1, block_rows - 1 - c, c)
        half = half_a if c < 4 else half_b
        value = start[pl.ds(pl.multiple_of(source * TILE, TILE), TILE), :]
        at = c % 4 * TILE
        half[at : at + TILE, :] = value[:, :TILE]
        half[HALF + at : HALF + at + TILE, :] = value[:, TILE:]

def halve(info, start):
    vmem = pl.BlockSpec(memory_space=pltpu.VMEM)
    half = jax.ShapeDtypeStruct((2 * HALF, TILE), start.dtype)
    return pl.pallas_call(
        halve_kernel,
        out_shape=(half, half),
        in_specs=[pl.BlockSpec(memory_space=pltpu.SMEM), vmem],
        out_specs=(vmem, vmem),
        compiler_params=pltpu.CompilerParams(vmem_limit_bytes=8 * 1024 * 1024),
        name="halve_start",
    )(info, start)

def swap_kernel(info, *refs):
    operators, swapped = refs[:-1], refs[-1]
    span = operators[0].shape[0]
    for n, (operator, following) in enumerate(zip(operators[:-1], operators[1:])):
        @pl.loop(0, span, step=160)
        def _(line):
            at = pl.ds(pl.multiple_of(line, 32), 160)
            to = pl.ds(pl.multiple_of(n * span + line, 32), 160)
            swapped[to, :] = jnp.where(info[2] == 0, following[at, :], operator[at, :])

def gather_swap(info, operators):
    vmem = pl.BlockSpec(memory_space=pltpu.VMEM)
    lines = (len(operators) - 1) * operators[0].shape[0]
    return pl.pallas_call(
        swap_kernel,
        out_shape=jax.ShapeDtypeStruct((lines, TILE), operators[0].dtype),
        in_specs=[pl.BlockSpec(memory_space=pltpu.SMEM)] + [vmem] * len(operators),
        out_specs=vmem,
        compiler_params=pltpu.CompilerParams(vmem_limit_bytes=24 * 1024 * 1024),
        name="gather_swap",
    )(info, *operators)


NB = 32

def factor_kernel(info, gram_ref, half_a, half_b, basis_ref, factor_ref, a_ref, w_ref):
    size = gram_ref.shape[0]
    a_ref[...] = gram_ref[...]
    row_i = lax.broadcasted_iota(jnp.int32, (size, size), 0)
    col_i = lax.broadcasted_iota(jnp.int32, (size, size), 1)
    w_ref[...] = jnp.where(row_i == col_i, 1.0, 0.0)
    lanes = 128
    sub = lax.broadcasted_iota(jnp.int32, (NB, lanes), 0)
    wide_row = lax.broadcasted_iota(jnp.int32, (NB, size), 0)
    wide_col = lax.broadcasted_iota(jnp.int32, (NB, size), 1)
    for first in range(0, size, NB):
        panel = a_ref[first : first + NB, :]
        other = w_ref[first : first + NB, :]
        columns = [
            jnp.broadcast_to(panel[:, first + k : first + k + 1], (NB, lanes))
            for k in range(NB)
        ]
        pivots = jnp.zeros((NB, lanes), jnp.float32)
        for j in range(NB):
            column = columns[j]
            pivot = jnp.broadcast_to(column[j : j + 1, :], (NB, lanes))
            pivots = jnp.where(sub == j, pivot, pivots)
            if j == NB - 1:
                break
            scaled = jnp.where(sub > j, column / pivot, 0.0)
            for k in range(j + 1, NB):
                columns[k] = columns[k] - scaled * jnp.broadcast_to(
                    column[k : k + 1, :], (NB, lanes)
                )
            both = jnp.concatenate([scaled] * (size // lanes), axis=1)
            panel = panel - both * jnp.broadcast_to(panel[j : j + 1, :], (NB, size))
            other = other - both * jnp.broadcast_to(other[j : j + 1, :], (NB, size))
        scale = 1.0 / jnp.sqrt(pivots)
        both = jnp.concatenate([scale] * (size // lanes), axis=1)
        upper = jnp.where(wide_col >= wide_row + first, panel * both, 0.0)
        other = other * both
        factor_ref[first : first + NB, :] = upper
        w_ref[first : first + NB, :] = other
        rest = first + NB
        if rest < size:
            low_row = rest // lanes * lanes
            low_lane = first // lanes * lanes
            high_lane = low_lane + lanes
            right = jnp.concatenate([upper[:, low_lane:], other[:, :high_lane]], axis=1)
            change = lax.dot_general(
                upper[:, low_row:], right, (((0,), (0,)), ((), ())),
                preferred_element_type=jnp.float32, precision=lax.Precision.HIGHEST,
            )[rest - low_row :, :]
            split = size - low_lane
            a_ref[rest:, low_lane:] = a_ref[rest:, low_lane:] - change[:, :split]
            w_ref[rest:, :high_lane] = w_ref[rest:, :high_lane] - change[:, split:]
    w = w_ref[...]
    high = w.astype(jnp.bfloat16)
    low = (w - high.astype(jnp.float32)).astype(jnp.bfloat16)
    dims = (((1,), (1,)), ((), ()))
    for c in range(8):
        half = half_a if c < 4 else half_b
        rows = half[c % 4 * TILE : (c % 4 + 1) * TILE, :]
        place = jnp.where(info[0] == 1, 7 - c, c)
        basis_ref[pl.ds(pl.multiple_of(place * TILE, TILE), TILE), :] = lax.dot_general(
            rows, high, dims, preferred_element_type=jnp.float32
        ) + lax.dot_general(rows, low, dims, preferred_element_type=jnp.float32)

def finish(info, gram, halves):
    size = gram.shape[0]
    vmem = pl.BlockSpec(memory_space=pltpu.VMEM)
    return pl.pallas_call(
        factor_kernel,
        out_shape=(
            jax.ShapeDtypeStruct((2 * HALF, size), jnp.float32),
            jax.ShapeDtypeStruct((size, size), jnp.float32),
        ),
        in_specs=[pl.BlockSpec(memory_space=pltpu.SMEM), vmem, vmem, vmem],
        out_specs=(vmem, vmem),
        scratch_shapes=[pltpu.VMEM((size, size), jnp.float32), pltpu.VMEM((size, size), jnp.float32)],
        name="factor_solve",
    )(info, gram, *halves)


def sum_over_rows(term):
    owners = lax.axis_size("rows")
    size = term.shape[0]
    pieces = term.reshape(owners, size // owners, size)
    pieces = lax.all_to_all(pieces, "rows", 0, 0, tiled=True)
    mine = jnp.sum(pieces.astype(jnp.float32), axis=0, keepdims=True)
    copies = jnp.broadcast_to(mine, (owners, size // owners, size))
    return lax.all_to_all(copies, "rows", 0, 0, tiled=True).reshape(size, size)


def body(start, blocks, cols, counts):
    block_rows, _, _ = blocks.shape[1:4]
    rows_here = start.shape[1]
    owners = lax.axis_size("rows")
    sections = lax.axis_size("phase")
    place = lax.axis_index("rows")
    core = lax.axis_index("phase") % 2
    info = jnp.stack([1 - place % 2, place * block_rows, core]).astype(jnp.int32)
    first_core = core == 0
    to_a = [(i, i ^ 1) for i in range(owners)]
    to_b = [(i, (i + 1) % owners if i % 2 else (i - 1) % owners) for i in range(owners)]
    back = [(i, (i - 2) % sections) for i in range(sections)]
    ahead = [(i, (i + 2) % sections) for i in range(sections)]
    mates = [(i, i ^ 1) for i in range(sections)]

    def rims(a_side, b_side):
        return (lax.ppermute(a_side, "rows", to_a), lax.ppermute(b_side, "rows", to_b))

    visits = sections // 2
    far = visits // 2
    home, home_a, home_b = pack(block_rows * owners, info, cols[0], counts[0], blocks[0])
    held = {0: home, visits: home}
    held[1] = lax.ppermute(home, "phase", back)
    held[visits - 1] = lax.ppermute(home, "phase", ahead)
    halves = halve(info, start[0])
    first_rims = rims(home_a, home_b)
    span = home.shape[0]
    rim_span = home_a.shape[0]
    riders = {n: [n] for n in range(1, far + 2)}
    for n in range(far + 2, visits):
        riders[visits - n].append(n)
    rim_of = {0: (first_rims, 0)}
    for turn in range(visits):
        sides = (lax.ppermute(halves[0], "rows", to_a), lax.ppermute(halves[1], "rows", to_b))
        second_at = 0
        if turn <= far:
            here, later, halves = lax.optimization_barrier((held[turn], held[turn + 1], halves))
            if turn + 2 <= far:
                held[turn + 2] = lax.ppermute(later, "phase", back)
            end = visits - 2 - turn
            if end > far:
                nearer, halves = lax.optimization_barrier((held[end + 1], halves))
                held[end] = lax.ppermute(nearer, "phase", ahead)
            picked = jnp.where(first_core, later, here)
            other = lax.ppermute(picked, "phase", mates)
        if turn == far:
            last = [later] + [held[n] for n in range(turn + 2, visits)] + [home]
            others = lax.ppermute(gather_swap(info, last), "phase", mates)
        if turn > far:
            other, second_at = others, (turn - far - 1) * span
        for n, operator in enumerate(riders.get(turn, [])):
            rim_of[operator] = (sides, rows_here + n * rim_span)
        rim, rim_at = rim_of[turn]
        following = [held[n] for n in riders.get(turn + 1, [])]
        halves = visit(
            halves, sides, rim, held[turn], other, following,
            turn + 1 == visits, rim_at, second_at,
        )

    arrived = jnp.concatenate(halves, axis=0)
    gram_term = lax.dot_general(
        arrived, arrived, (((0,), (0,)), ((), ())), preferred_element_type=jnp.float32
    )
    gram_total = sum_over_rows(gram_term.astype(jnp.bfloat16)) / (rows_here * owners)
    basis_out, upper_factor = finish(info, gram_total, halves)
    return (basis_out[None], upper_factor[None])


def solution(mesh):
    placed = (
        P("phase", "rows", None),
        P("phase", "rows", None, None, None),
        P("phase", "rows", None),
        P("phase", "rows"),
    )
    return jax.shard_map(
        body,
        mesh=mesh,
        in_specs=placed,
        out_specs=(P("phase", "rows", None), P("phase", None, None)),
        check_vma=False,
    )
```
